512 devices in a mesh: view: 4 (over x), strip: 128 (over y, z, core).
Axes of the slice: x: 4, y: 8, z: 8, core: 2. Of those that a mesh axis runs over, the one named last changes fastest.
Arguments:
- means: float32 [3, 262144], P(None, 'strip'), may hold values from -4 to 4
- inv_scales: float32 [2, 262144], P(None, 'strip'), may hold values from 0.15 to 0.6
- correlation: float32 [262144], P('strip'), may hold values from -0.6 to 0.6
- opacity: float32 [262144], P('strip'), may hold values from -7 to 4
- features: float32 [262144, 128], P('strip'), may hold values from -48 to 48
- cameras: float32 [4, 2, 4], P('view'), may hold values from -0.8 to 0.8
- owners: int32 [4, 128, 256, 1], P('view', 'strip'), may hold values from 0 to 127; in each aligned block of 256 rows (0 to 255, 256 to 511, ..., all dimensions but the last counted through in order) at most 4 rows name the same one
- slots: int32 [4, 128, 256], P('view', 'strip'), may hold values from 0 to 2047
- lengths: int32 [4, 128], P('view', 'strip'), may hold values from 1 to 256, 20480 in all within a row
- target: float32 [4, 2048, 16, 128], P('view', 'strip'), may hold values from -6 to 6
- weights: float32 [3, 3, 128, 128], replicated, may hold values from -0.1875 to 0.1875
- bias: float32 [128], replicated, may hold values from -3 to 3
Outputs:
- geometry_grad: float32 [7, 262144], P(None, 'strip')
- feature_grad: float32 [262144, 128], P('strip')
- weight_grad: float32 [3, 3, 128, 128], replicated
- bias_grad: float32 [128], replicated
The draws below stay inside these ranges and needn't reach their ends.
Inputs may be any that keep to these rules, and one draw needn't show every extreme that they name: `owners`: in one device's entries (aligned blocks of 256 list entries in order of view, tile and position), no strip index is named more than 4 times; entries at or past a tile's length are padding but still name a primitive.
All inputs are finite; a program needn't handle non-finite values. No bound on the sum of `lengths` on one device may be relied on, other than what follows from the above.
Results may differ from the reference program's by a relative error of at most 0.0003.
Values sent between devices are 32-bit elements; how exact they have to be, the bound alone decides.
A program may use at most 64 MiB of HBM per device.

```python
import math
import jax
import jax.numpy as jnp
import numpy as np
from jax import lax

CH = 128
CAP = 256
TILES_DEV = 1
P_DEV = 2048
VIEWS = 4
TILES = 128
PRIMS = 262144
IMG_ROWS = 2048
IMG_COLS = 16
BUCKET = 4
N_STRIP = 128


def with_ends(array, key, low, high):
    longest = array.shape.index(max(array.shape))
    spots = []
    for shift in (0, 1):
        where = [jax.random.randint(jax.random.fold_in(key, axis), (), 0, length) for axis, length in enumerate(array.shape)]
        where[longest] = (where[longest] + shift) % array.shape[longest]
        spots.append(tuple(where))
    return array.at[spots[0]].set(low).at[spots[1]].set(high)


def block_scale(key, extent, cuts, smallest, high):
    def one(dim, parts):
        heights = jax.random.uniform(jax.random.fold_in(jax.random.fold_in(key, 6), dim), (parts,), jnp.float32, smallest / len(cuts), high / len(cuts))
        return jnp.repeat(jnp.exp(heights), extent[dim] // parts).reshape((-1,) + (1,) * (len(extent) - dim - 1))

    loudness = one(*cuts[0])
    for cut in cuts[1:]:
        loudness = loudness * one(*cut)
    return loudness


def length_profile(amount, total, most, skew):
    weights = [(1 << 20) // math.isqrt(standing ** skew) + 1 for standing in range(2, amount + 1)]
    rest, holding = total - most - (amount - 1), [1] * (amount - 1)
    while rest > 0:
        free = [i for i in range(amount - 1) if holding[i] < most]
        mass, remaining = sum([weights[i] for i in free]), rest
        for i in free:
            addition = min(most - holding[i], max(1, remaining * weights[i] // mass), rest)
            holding[i] = holding[i] + addition
            rest = rest - addition
    return np.array([most] + holding)


def ragged_sizes(stream_key, count, total, bound, slope):
    if count == 2:
        one = jax.random.randint(stream_key, (), max(1, total - bound), min(bound, total - 1) + 1)
        return jnp.stack([one, total - one])
    sizes = jnp.asarray(length_profile(count, total, bound, slope), jnp.int32)
    couples = (count - 1) // 2
    source_of, receiver = sizes[1:1 + 2 * couples:2], sizes[2:2 + 2 * couples:2]
    room = jnp.minimum(source_of - 1, bound - receiver)
    passed = jax.random.randint(jax.random.fold_in(stream_key, 1), (couples,), 0, 1 << 20) % (room + 1)
    sizes = sizes.at[1:1 + 2 * couples:2].set(source_of - passed).at[2:2 + 2 * couples:2].set(receiver + passed)
    return sizes[jax.random.permutation(jax.random.fold_in(stream_key, 2), count)]


def deal_out(key, own, number, rows, number_of, top, reach, lean):
    ranking = jax.random.permutation(key, number_of)
    crowded, usual = portions_of(number_of, rows * top, reach, lean, True), portions_of(number_of, rows * top, reach, lean, False)
    places = jnp.arange(number_of)

    def named(tallies, turn):
        used = int((tallies > 0).sum())
        fixed = max(1, used // 4)
        passed = fixed + (places - fixed + turn * (used - fixed)) % max(1, number_of - fixed)
        return jnp.zeros((number_of,), jnp.int32).at[ranking[jnp.where(places < fixed, places, passed)]].set(jnp.asarray(tallies, jnp.int32))

    tallies = jnp.where(number % 4 == 0, named(crowded, number // 4), named(usual, number - number // 4 - 1))
    mixed = jax.random.permutation(jax.random.fold_in(own, 3), number_of)
    donor, sink = mixed[0:number_of // 2 * 2:2], mixed[1:number_of // 2 * 2:2]
    slack = jnp.minimum(tallies[donor] - 1, reach - tallies[sink]) // 2
    slack = jnp.where((donor == ranking[0]) | (sink == ranking[0]) | (tallies[sink] == 0), 0, jnp.maximum(slack, 0))
    passed = jax.random.randint(jax.random.fold_in(own, 4), (number_of // 2,), 0, 1 << 20) % (slack + 1)
    tallies = tallies.at[donor].add(-passed).at[sink].add(passed)
    labels = jnp.searchsorted(jnp.cumsum(tallies), jnp.arange(rows * top), side="right").astype(jnp.int32)
    listing = labels.reshape(top, rows).T
    listing = listing[jax.random.permutation(jax.random.fold_in(own, 1), rows)]
    turn = jax.random.randint(jax.random.fold_in(own, 2), (rows, 1), 0, top)
    return jnp.take_along_axis(listing, (jnp.arange(top)[None, :] + turn) % top, axis=1)


def portions_of(count, total, bound, lean, full):
    weights = [(1 << 20) // math.isqrt(grade ** lean) + 1 for grade in range(1, count + 1)]
    largest = bound if full else min(bound, max(-(-total // count), total * weights[0] // sum(weights)))
    least = 1 if total - largest >= count - 1 else 0
    given, spare = [largest] + [least] * (count - 1), total - largest - least * (count - 1)
    while spare > 0:
        free = [i for i in range(1, count) if given[i] < largest] or [i for i in range(1, count) if given[i] < bound]
        mass, budget = sum([weights[i] for i in free]), spare
        for i in free:
            extra = min(bound - given[i], max(1, budget * weights[i] // mass), spare)
            given[i] = given[i] + extra
            spare = spare - extra
    return np.array(given)


def bell_draw(rng, extent, width, bound, pieces=(), kind=jnp.bfloat16):
    level = block_scale(rng, extent, pieces, -0.22, 0.18) if pieces else 1.0
    drawn = jax.random.normal(rng, extent, jnp.float32) * width * level
    return jnp.minimum(jnp.maximum(drawn, -bound), bound).astype(kind)


def setup_inputs(seed: int = 0) -> dict:
    key_list = jax.random.split(jax.random.key(seed), 13)
    means = bell_draw(key_list[0], (3, PRIMS), 1.0, 4.0, ((1, 128),), jnp.float32)
    inv_scales = jnp.clip(jnp.exp(math.log(0.6) - 1.3862944 * jax.random.uniform(key_list[1], (2, PRIMS), jnp.float32) ** block_scale(key_list[1], (2, PRIMS), ((1, 128),), -0.2, 0.2)), 0.15, 0.6)
    correlation = jnp.clip(jax.random.uniform(key_list[2], (PRIMS,), jnp.float32, -0.6, 0.6) * block_scale(key_list[2], (PRIMS,), ((0, 128),), -0.4, 0.0), -0.6, 0.6)
    opacity = jnp.clip(-7.0 + 11.0 * jax.random.uniform(key_list[3], (PRIMS,), jnp.float32) ** block_scale(key_list[3], (PRIMS,), ((0, 128),), -0.2, 0.2), -7.0, 4.0)
    features = bell_draw(key_list[4], (PRIMS, CH), 8.0, 48.0, ((0, 128),), jnp.float32)
    cameras = jnp.clip(jax.random.uniform(key_list[5], (VIEWS, 2, 4), jnp.float32, -0.8, 0.8) * block_scale(key_list[5], (VIEWS, 2, 4), ((0, 4),), -0.4, 0.0), -0.8, 0.8)
    owners_keys = jax.random.split(jax.random.fold_in(key_list[6], 1), VIEWS * TILES * CAP // (TILES_DEV * CAP))
    owners_turns = jax.random.permutation(jax.random.fold_in(key_list[6], 3), VIEWS * TILES * CAP // (TILES_DEV * CAP))
    owners = jax.vmap(lambda own, number: deal_out(jax.random.fold_in(key_list[6], 2), own, number, TILES_DEV * CAP, N_STRIP, 1, BUCKET, 2))(owners_keys, owners_turns).reshape((VIEWS, TILES, CAP, 1))
    slots = with_ends(jax.random.randint(key_list[7], (VIEWS, TILES, CAP), 0, P_DEV), jax.random.fold_in(key_list[7], 1), 0, P_DEV - 1).astype(jnp.int32)
    lengths = jax.vmap(lambda own: ragged_sizes(own, TILES, (TILES * CAP * 5) // 8, CAP, 2))(jax.random.split(key_list[8], VIEWS)).reshape((VIEWS, TILES)).astype(jnp.int32)
    target = bell_draw(key_list[9], (VIEWS, IMG_ROWS, IMG_COLS, CH), 1.0, 6.0, ((0, 4), (1, 128)), jnp.float32)
    weights = bell_draw(key_list[10], (3, 3, CH, CH), (9 * CH) ** -0.5, 0.1875, (), jnp.float32)
    bias = bell_draw(key_list[11], (CH,), 0.5, 3.0, (), jnp.float32)
    return dict(means=means, inv_scales=inv_scales, correlation=correlation, opacity=opacity, features=features, cameras=cameras, owners=owners, slots=slots, lengths=lengths, target=target, weights=weights, bias=bias)


HIGHEST = lax.Precision.HIGHEST

def render_tile(geometry, feature, length, camera):
    entries = geometry.shape[0]
    pixels = jnp.arange(256, dtype=jnp.int32)
    across = (pixels % 16).astype(jnp.float32) + 0.5
    downward = (pixels // 16).astype(jnp.float32) + 0.5
    center_col = 8.0 + 4.0 * (camera[0, 0] * geometry[:, 0] + camera[0, 1] * geometry[:, 1] + camera[0, 2] * geometry[:, 2] + camera[0, 3])
    center_row = 8.0 + 4.0 * (camera[1, 0] * geometry[:, 0] + camera[1, 1] * geometry[:, 1] + camera[1, 2] * geometry[:, 2] + camera[1, 3])
    scaled_col = geometry[:, 3][None, :] * (across[:, None] - center_col[None, :])
    scaled_row = geometry[:, 4][None, :] * (downward[:, None] - center_row[None, :])
    exponent = -0.5 * (scaled_col * scaled_col + 2.0 * geometry[:, 5][None, :] * scaled_col * scaled_row + scaled_row * scaled_row)
    alive_mask = (jnp.arange(entries, dtype=jnp.int32) < length).astype(jnp.float32)
    coverage = jnp.minimum(jax.nn.sigmoid(geometry[:, 6])[None, :] * jnp.exp(exponent), 0.99) * alive_mask[None, :]
    log_keep = jnp.log1p(-coverage)
    transmit = jnp.exp(jnp.cumsum(log_keep, axis=1) - log_keep)
    return jnp.dot(coverage * transmit, feature, precision=HIGHEST)

def convolve(padded, kernel, height, breadth):
    channels = padded.shape[-1]
    total = jnp.zeros((height * breadth, kernel.shape[-1]), jnp.float32)
    for tap_row in range(3):
        for tap_col in range(3):
            piece = padded[tap_row:tap_row + height, tap_col:tap_col + breadth].reshape(height * breadth, channels)
            total = total + jnp.dot(piece, kernel[tap_row, tap_col], precision=HIGHEST)
    return total

def reference(means, inv_scales, correlation, opacity, features, cameras, owners, slots, lengths, target, weights, bias):
    table = jnp.concatenate([means, inv_scales, correlation[None, :], opacity[None, :]], axis=0).T
    index = owners[..., 0] * P_DEV + slots
    height = target.shape[1]
    breadth = target.shape[2]
    channels = target.shape[3]
    geometry_total = jnp.zeros(table.shape, jnp.float32)
    feature_total = jnp.zeros(features.shape, jnp.float32)
    kernel_total = jnp.zeros(weights.shape, jnp.float32)
    bias_total = jnp.zeros(bias.shape, jnp.float32)
    flipped = jnp.transpose(weights[::-1, ::-1], (0, 1, 3, 2))
    for view in range(VIEWS):
        picked = index[view]
        geometry = table[picked]
        feature = features[picked]
        camera = cameras[view]
        view_lengths = lengths[view]

        def render_all(geometry, feature):

            def single(packed):
                return render_tile(packed[0], packed[1], packed[2], camera)
            return lax.map(jax.checkpoint(single), (geometry, feature, view_lengths))
        tiles, pullback = jax.vjp(render_all, geometry, feature)
        image = tiles.reshape(N_STRIP, TILES_DEV, 16, 16, channels).transpose(0, 2, 1, 3, 4).reshape(height, breadth, channels)
        padded = jnp.pad(image, ((1, 1), (1, 1), (0, 0)))
        decoded = convolve(padded, weights, height, breadth) + bias[None, :]
        residual = decoded - target[view].reshape(height * breadth, channels)
        tap_terms = []
        for tap_row in range(3):
            for tap_col in range(3):
                piece = padded[tap_row:tap_row + height, tap_col:tap_col + breadth].reshape(height * breadth, channels)
                tap_terms.append(jnp.dot(piece.T, residual, precision=HIGHEST))
        kernel_total = kernel_total + jnp.stack(tap_terms).reshape(3, 3, channels, channels)
        bias_total = bias_total + lax.optimization_barrier(jnp.sum(residual, axis=0))
        beside_all = jnp.pad(residual.reshape(height, breadth, channels), ((1, 1), (1, 1), (0, 0)))
        image_grad = convolve(beside_all, flipped, height, breadth)
        tile_grad = image_grad.reshape(N_STRIP, 16, TILES_DEV, 16, channels).transpose(0, 2, 1, 3, 4).reshape(TILES, 256, channels)
        geometry_grad, feature_grad = pullback(tile_grad)
        flat_index = picked.reshape(-1)
        geometry_total = geometry_total.at[flat_index].add(geometry_grad.reshape(-1, 7))
        feature_total = feature_total.at[flat_index].add(feature_grad.reshape(-1, channels))
    return (geometry_total.T, feature_total, kernel_total, bias_total)
```

```python
import functools

import jax
import jax.numpy as jnp
from jax import lax
from jax.experimental import pallas as pl
from jax.experimental.pallas import tpu as pltpu
from jax.sharding import Mesh
from jax.sharding import PartitionSpec as P

STRIP = ("strip_0", "strip_1", "strip_2")
MESH = pl.DeviceIdType.MESH
F32 = jnp.float32
BF16 = jnp.bfloat16
RANKS = 4


def iota(shape, dim):
    return lax.broadcasted_iota(jnp.int32, shape, dim)


def mm(a, b, ca=1, cb=0):
    return lax.dot_general(a, b, (((ca,), (cb,)), ((), ())), preferred_element_type=F32)


def split(x):
    high = x.astype(BF16)
    return high, (x - high.astype(F32)).astype(BF16)


def split3(x):
    high = x.astype(BF16)
    rest = x - high.astype(F32)
    mid = rest.astype(BF16)
    return high, mid, (rest - mid.astype(F32)).astype(BF16)


def rows_of(ref, n):
    return ref.reshape(n, ref.shape[-1])[...]


def fill(ref, value):
    ref.reshape(*value.shape)[...] = value


def kernel(
    sizes,
    means, inv_scales, correlation, opacity, cameras, owners, slots, lengths, bias,
    features_hbm, target_hbm, weights_hbm,
    geometry_out, feature_out, weight_out, bias_out,
    feat, targ, wts, table, g_parts, f_parts, w_parts, w_turned, onehot, halo_t,
    req, req_mid, req_got, asked_all,
    geo, geo_mid, geo_got, fea, fea_mid, fea_got,
    image, back, back_mid, back_got, bgeo, bgeo_mid, bgeo_got, all_f, all_g,
    total, wl, wx, wc, wz, wz_got, wy, wy_got, wq, wq_got, wa, wfin,
    send, recv, local,
):
    nx, ny, nz, nc, entries, prims, height = sizes
    zc_count = nz * nc
    strips = ny * zc_count
    places = RANKS * strips
    width = 128
    pixels = height * 16
    extended = pixels + 32
    v = lax.axis_index("view")
    y = lax.axis_index("strip_0")
    z = lax.axis_index("strip_1")
    c = lax.axis_index("strip_2")
    zc = z * nc + c
    strip = y * zc_count + zc

    def at_zc(k):
        return (v, y, k // nc, k % nc)

    def at_y(k):
        return (v, k, z, c)

    def at_x(k):
        return (k, y, z, c)

    def at_strip(k):
        return (v, k // zc_count, (k % zc_count) // nc, k % nc)

    up = at_strip((strip + strips - 1) % strips)
    down = at_strip((strip + 1) % strips)

    def push(src, dst, n, device):
        pltpu.make_async_remote_copy(
            src_ref=src, dst_ref=dst, send_sem=send.at[n], recv_sem=recv.at[n],
            device_id=device, device_id_type=MESH,
        ).start()

    def keep(src, dst, n):
        pltpu.make_async_copy(src, dst, recv.at[n]).start()

    def landed(ref, n):
        pltpu.make_async_copy(ref, ref, recv.at[n]).wait()

    def sent(ref, n):
        pltpu.make_async_copy(ref, ref, send.at[n]).wait()

    pending = []

    def to_zc(src, dst, n):
        @pl.loop(1, zc_count)
        def _(j):
            k = (zc + j) % zc_count
            push(src.at[:, k], dst.at[:, zc], n, at_zc(k))

        keep(src.at[:, zc], dst.at[:, zc], n)
        pending.append((src.at[:, 0 : zc_count - 1], n))

    def to_y(src, dst, n):
        @pl.loop(1, ny)
        def _(j):
            k = (y + j) % ny
            push(src.at[:, :, k], dst.at[:, :, y], n, at_y(k))

        keep(src.at[:, :, y], dst.at[:, :, y], n)
        pending.append((src.at[:, :, 0 : ny - 1], n))

    load_f = pltpu.make_async_copy(features_hbm, feat, local.at[0])
    load_t = pltpu.make_async_copy(target_hbm, targ, local.at[1])
    load_w = pltpu.make_async_copy(weights_hbm, wts, local.at[2])
    load_f.start()
    load_t.start()
    load_w.start()

    barrier = pltpu.get_barrier_semaphore()

    @pl.loop(1, zc_count)
    def _(j):
        pl.semaphore_signal(barrier, inc=1, device_id=at_zc((zc + j) % zc_count), device_id_type=MESH)

    @pl.loop(1, ny)
    def _(j):
        pl.semaphore_signal(barrier, inc=1, device_id=at_y((y + j) % ny), device_id_type=MESH)

    @pl.loop(1, nx)
    def _(j):
        pl.semaphore_signal(barrier, inc=1, device_id=at_x((v + j) % nx), device_id_type=MESH)

    pl.semaphore_signal(barrier, inc=1, device_id=up, device_id_type=MESH)
    pl.semaphore_signal(barrier, inc=1, device_id=down, device_id_type=MESH)

    def column(row):
        n = row.shape[1]
        same = iota((n, n), 0) == iota((n, n), 1)
        return jnp.sum(jnp.where(same, jnp.broadcast_to(row, (n, n)), 0.0), axis=1, keepdims=True)

    owner = owners[...]
    home = ((owner % zc_count) * ny + owner // zc_count).astype(F32)
    home_col = column(home)
    slot_col = column(slots[...].astype(F32))
    alike = home_col == home
    first = iota((entries, entries), 0)
    second = iota((entries, entries), 1)
    rank_col = jnp.sum(jnp.where(alike & (second < first), 1.0, 0.0), axis=1, keepdims=True)
    rank_row = jnp.sum(jnp.where(alike & (first < second), 1.0, 0.0), axis=0, keepdims=True)
    at_home = jnp.where(iota((strips, entries), 0).astype(F32) == home, 1.0, 0.0).astype(BF16)
    lane = iota((entries, width), 1).astype(F32)
    slot_high = jnp.floor(slot_col * (1.0 / 64.0))
    slot_low = slot_col - 64.0 * slot_high
    in_rank = lane == rank_col
    asked_high = mm(at_home, jnp.where(in_rank, slot_high, 0.0).astype(BF16))
    asked_low = mm(at_home, jnp.where(in_rank, slot_low, 0.0).astype(BF16))
    fill(req, asked_high * 64.0 + asked_low)

    pl.semaphore_wait(barrier, zc_count + ny + nx - 3 + 2)

    to_zc(req, req_mid, 0)
    push(target_hbm.at[0:16], halo_t.at[1], 1, up)
    push(target_hbm.at[pixels - 16 : pixels], halo_t.at[0], 1, down)
    pending.append((halo_t, 1))

    table[0:3, :] = means[...]
    table[3:5, :] = inv_scales[...]
    table[5:6, :] = correlation[...]
    table[6:7, :] = opacity[...]
    table[7:8, :] = jnp.zeros((1, prims), F32)
    whole = table[...]
    g_high, g_mid, g_low = (part.astype(F32) for part in split3(whole))
    g_parts[...] = jnp.concatenate(
        [g_high] * RANKS + [g_mid] * RANKS + [g_low] * RANKS + [jnp.zeros((32, prims), F32)], axis=0
    ).astype(BF16)
    load_f.wait()
    rows = min(prims, 256)

    @pl.loop(0, prims // rows)
    def _(i):
        here = pl.ds(pl.multiple_of(i * rows, rows), rows)
        high, low = split(feat[here, :])
        f_parts[here, 0:width] = high
        f_parts[here, width : 2 * width] = low

    landed(req_mid, 0)
    to_y(req_mid, req_got, 2)

    load_w.wait()
    for tap in range(9):
        high, low = split(wts[tap * width : (tap + 1) * width, :])
        w_parts[tap * width : (tap + 1) * width, 0:width] = high
        w_parts[tap * width : (tap + 1) * width, width : 2 * width] = low
        a, b = 2 - tap // 3, 2 - tap % 3
        w_turned[a, 0, :, b * width : (b + 1) * width] = high
        w_turned[a, 1, :, b * width : (b + 1) * width] = low
    load_t.wait()

    landed(req_got, 2)
    asked = rows_of(req_got, strips)
    square = jnp.concatenate([asked, jnp.zeros((width - strips, width), F32)], axis=0) if strips < width else asked
    asked_rows = jnp.transpose(square)[0:8, 0:strips]
    asked_all[v] = asked_rows

    @pl.loop(1, nx)
    def _(j):
        push(asked_all.at[v], asked_all.at[v], 3, at_x((v + j) % nx))

    if nx > 1:
        pending.append((asked_all.at[0 : nx - 1], 3))

    ident = iota((strips, prims), 1).astype(F32)
    packed = jnp.zeros((strips, width), F32)
    lanes = iota((strips, width), 1)
    for r in range(RANKS):
        onehot[r * strips : (r + 1) * strips, :] = jnp.where(ident == asked[:, r : r + 1], 1.0, 0.0).astype(BF16)
    for r in range(RANKS):
        found = mm(onehot[r * strips : (r + 1) * strips, :], g_parts[...], 1, 1)
        packed = packed + jnp.where((lanes % 32) // 8 == r, found, 0.0)

    def folded(x):
        x = x + pltpu.roll(x, width - 32, 1) + pltpu.roll(x, width - 64, 1)
        return jnp.where(lanes < 32, x, 0.0)

    fill(geo, folded(packed))
    to_zc(geo, geo_mid, 4)

    @pl.loop(0, RANKS)
    def _(r):
        here = pl.ds(pl.multiple_of(r * strips, strips), strips)
        found = mm(onehot[here, :], f_parts[...])
        fill(fea.at[r], found[:, 0:width] + found[:, width : 2 * width])

    half = RANKS // 2
    to_zc(fea.at[0:half], fea_mid.at[0:half], 5)
    to_y(fea.at[half:RANKS], fea_mid.at[half:RANKS], 6)

    landed(geo_mid, 4)
    to_y(geo_mid, geo_got, 7)

    place_row = rank_row * float(strips) + home
    place_col = rank_col * float(strips) + home_col
    to_place = jnp.where(iota((places, entries), 0).astype(F32) == place_row, 1.0, 0.0).astype(BF16)
    from_place = jnp.where(iota((entries, places), 1).astype(F32) == place_col, 1.0, 0.0).astype(BF16)
    before = jnp.where(first < second, 1.0, 0.0).astype(BF16)
    behind = jnp.where(first > second, 1.0, 0.0).astype(BF16)

    landed(fea_mid.at[0:half], 5)
    to_y(fea_mid.at[0:half], fea_got.at[0:half], 8)
    landed(fea_mid.at[half:RANKS], 6)
    to_zc(fea_mid.at[half:RANKS], fea_got.at[half:RANKS], 9)

    landed(geo_got, 7)

    def turned(x):
        x = jnp.concatenate([x, jnp.zeros((width - strips, width), F32)], axis=0) if strips < width else x
        return jnp.transpose(x)[0 : 8 * RANKS, 0:strips]

    def three(x):
        return jnp.concatenate([part.astype(F32) for part in split3(x)], axis=0).astype(BF16)

    spread = mm(three(turned(rows_of(geo_got, strips))), at_home)
    n8 = 8 * RANKS
    spread = spread[0:n8] + spread[n8 : 2 * n8] + spread[2 * n8 : 3 * n8]
    g = jnp.zeros((8, entries), F32)
    for r in range(RANKS):
        g = g + jnp.where(rank_row == float(r), spread[8 * r : 8 * r + 8, :], 0.0)

    def cam(axis, k):
        return cameras[0, axis * 4 + k]

    def center(axis):
        return 8.0 + 4.0 * (
            cam(axis, 0) * g[0:1] + cam(axis, 1) * g[1:2] + cam(axis, 2) * g[2:3] + cam(axis, 3)
        )

    pixel = iota((pixels, 1), 0)
    across = (pixel % 16).astype(F32) + 0.5
    downward = (pixel // 16).astype(F32) + 0.5
    du = across - center(0)
    dv = downward - center(1)
    a = g[3:4] * du
    b = g[4:5] * dv
    skew = g[5:6]
    grown = jnp.exp(-0.5 * (a * a + 2.0 * skew * a * b + b * b))
    solid = 1.0 / (1.0 + jnp.exp(-g[6:7]))
    raw = solid * grown
    alive = jnp.where(iota((1, entries), 1) < lengths[0, 0], 1.0, 0.0)
    cover = jnp.minimum(raw, 0.99) * alive
    fades = jnp.log(1.0 - cover)
    f_high, f_mid, f_low = split3(fades)
    through = jnp.exp(mm(f_high, before) + mm(f_mid, before) + mm(f_low, before))
    weight = cover * through
    weight_high, weight_low = split(weight)

    landed(fea_got.at[0:half], 8)
    landed(fea_got.at[half:RANKS], 9)
    high, low = split(rows_of(fea_got, places))
    listed = mm(from_place, jnp.concatenate([high, low], axis=1)).astype(BF16)
    both = mm(weight_high, listed)
    image[32 : 32 + pixels, :] = both[:, 0:width] + both[:, width:] + mm(weight_low, listed[:, 0:width])

    push(image.at[32:64], image.at[32 + pixels : 64 + pixels], 10, up)
    push(image.at[pixels : 32 + pixels], image.at[0:32], 10, down)
    pending.append((image.at[0:64], 10))
    landed(image.at[0:64], 10)
    landed(halo_t, 1)

    has_up = strip > 0
    has_down = strip < strips - 1
    rows_at = iota((pixels + 64, 1), 0)
    inside = ((rows_at >= 32) | has_up) & ((rows_at < 32 + pixels) | has_down)
    pic = jnp.where(inside, image[...], 0.0)

    def sideways(x):
        n = x.shape[0]
        col = iota((n, 1), 0) % 16
        left = jnp.where(col == 0, 0.0, pltpu.roll(x, 1, 0))
        right = jnp.where(col == 15, 0.0, pltpu.roll(x, n - 1, 0))
        return split(jnp.concatenate([left, x, right], axis=1))

    pic_high, pic_low = sideways(pic)
    decoded = jnp.zeros((extended, 2 * width), F32)
    rest = jnp.zeros((extended, width), F32)
    for i in range(3):
        part = w_parts[i * 3 * width : (i + 1) * 3 * width, :]
        decoded = decoded + mm(pic_high[i * 16 : i * 16 + extended, :], part)
        rest = rest + mm(pic_low[i * 16 : i * 16 + extended, :], part[:, 0:width])
    decoded = decoded[:, 0:width] + (decoded[:, width:] + rest) + bias[...]
    aim = jnp.concatenate([halo_t[0], targ[...], halo_t[1]], axis=0)
    rows_at = iota((extended, 1), 0)
    inside = ((rows_at >= 16) | has_up) & ((rows_at < 16 + pixels) | has_down)
    residual = jnp.where(inside, decoded - aim, 0.0)
    res_high, res_low = sideways(residual)
    grad = jnp.zeros((pixels, width), F32)
    for i in range(3):
        here = slice(i * 16, i * 16 + pixels)
        grad = grad + (
            mm(res_high[here, :], w_turned[i, 0], 1, 1)
            + (mm(res_high[here, :], w_turned[i, 1], 1, 1) + mm(res_low[here, :], w_turned[i, 0], 1, 1))
        )
    grad_high, grad_low = split(grad)

    both = mm(weight_high, jnp.concatenate([grad_high, grad_low], axis=1), 0, 0)
    f_grad = both[:, 0:width] + (both[:, width:] + mm(weight_low, grad_high, 0, 0))
    high, low = split(f_grad)
    both = mm(to_place, jnp.concatenate([high, low], axis=1))
    fill(back, both[:, 0:width] + both[:, width:])
    to_zc(back.at[0:half], back_mid.at[0:half], 11)
    to_y(back.at[half:RANKS], back_mid.at[half:RANKS], 12)

    own = residual[16 : 16 + pixels, :]
    shifted = []
    for i in range(3):
        shifted.append(
            jnp.concatenate(
                [jnp.zeros(((i + 1) * 16, width), F32), own, jnp.zeros((64 - (i + 1) * 16, width), F32)], axis=0
            )
        )
    own_high, own_low = split(jnp.concatenate(shifted, axis=1))
    w_grad = mm(pic_high, own_high, 0, 0) + (mm(pic_high, own_low, 0, 0) + mm(pic_low, own_high, 0, 0))
    for i in range(3):
        wl[i * 3 * width : (i + 1) * 3 * width, :] = w_grad[:, i * width : (i + 1) * width]
    b_grad = jnp.broadcast_to(jnp.sum(own, axis=0, keepdims=True), (8, width))
    per_z = 9 * width // zc_count
    per_y = per_z // ny
    for k in range(zc_count):
        wx[k // nz, k % nz, 0:per_z, :] = wl[k * per_z : (k + 1) * per_z, :]
        wx[k // nz, k % nz, per_z : per_z + 8, :] = b_grad
    other = (v, y, z, 1 - c)
    push(wx.at[1 - c], wc, 13, other)
    pending.append((wc, 13))

    d_weight = mm(jnp.concatenate([grad_high, grad_high], axis=1), listed, 1, 1) + mm(
        grad_low, listed[:, 0:width], 1, 1
    )
    f_high, f_mid, f_low = split3(d_weight * weight)
    later = mm(f_high, behind) + mm(f_mid, behind) + mm(f_low, behind)
    d_cover = d_weight * through - later / (1.0 - cover)
    d_raw = jnp.where(raw < 0.99, d_cover, 0.0) * alive
    d_grown = d_raw * raw
    u = (a + skew * b) * d_grown
    w = (b + skew * a) * d_grown

    def summed(x):
        return jnp.sum(x, axis=0, keepdims=True)

    d_col = 4.0 * g[3:4] * summed(u)
    d_row = 4.0 * g[4:5] * summed(w)
    parts = [cam(0, k) * d_col + cam(1, k) * d_row for k in range(3)]
    parts += [-summed(u * du), -summed(w * dv), -summed(d_grown * a * b), summed(d_grown) * (1.0 - solid)]
    parts.append(jnp.zeros((1, entries), F32))
    g_grad = jnp.concatenate(parts, axis=0)
    by_rank = jnp.concatenate([jnp.where(rank_row == float(r), g_grad, 0.0) for r in range(RANKS)], axis=0)
    by_rank = jnp.concatenate([part.astype(F32) for part in split3(by_rank)] + [jnp.zeros((32, entries), F32)], axis=0)
    fill(bgeo, folded(mm(at_home, by_rank.astype(BF16), 1, 1)))
    to_zc(bgeo, bgeo_mid, 14)

    landed(wc, 13)
    wz[...] = wx[c] + wc[...]

    @pl.loop(1, nz)
    def _(j):
        k = (z + j) % nz
        push(wz.at[k], wz_got.at[z], 15, (v, y, k, c))

    keep(wz.at[z], wz_got.at[z], 15)
    pending.append((wz.at[0 : nz - 1], 15))

    landed(back_mid.at[0:half], 11)
    to_y(back_mid.at[0:half], back_got.at[0:half], 16)
    landed(back_mid.at[half:RANKS], 12)
    to_zc(back_mid.at[half:RANKS], back_got.at[half:RANKS], 17)
    landed(bgeo_mid, 14)
    to_y(bgeo_mid, bgeo_got, 18)

    landed(wz_got, 15)
    sums = wz_got[0]
    for k in range(1, nz):
        sums = sums + wz_got[k]
    for k in range(ny):
        fill(wy.at[k, 0:per_y], sums[k * per_y : (k + 1) * per_y, :])
        fill(wy.at[k, per_y : per_y + 1], sums[per_z : per_z + 1, :])

    @pl.loop(1, ny)
    def _(j):
        k = (y + j) % ny
        push(wy.at[k], wy_got.at[y], 19, at_y(k))

    keep(wy.at[y], wy_got.at[y], 19)
    pending.append((wy.at[0 : ny - 1], 19))

    def to_x(src, dst, n):
        @pl.loop(1, nx)
        def _(j):
            push(src, dst, n, at_x((v + j) % nx))

        keep(src, dst, n)
        for _ in range(nx - 1):
            pending.append((src, n))

    landed(back_got.at[0:half], 16)
    to_x(back_got.at[0:half], all_f.at[v, 0:half], 20)
    landed(back_got.at[half:RANKS], 17)
    to_x(back_got.at[half:RANKS], all_f.at[v, half:RANKS], 21)
    landed(bgeo_got, 18)
    to_x(bgeo_got, all_g.at[v], 22)

    landed(wy_got, 19)
    sums = wy_got[0]
    for k in range(1, ny):
        sums = sums + wy_got[k]
    wq[...] = sums
    to_x(wq, wq_got.at[v], 23)

    if nx > 1:
        landed(asked_all.at[0 : nx - 1], 3)
    landed(wq_got, 23)
    sums = wq_got[0]
    for k in range(1, nx):
        sums = sums + wq_got[k]
    bias_out[...] = sums[per_y]
    wa[y] = sums[0:per_y]

    @pl.loop(1, ny)
    def _(j):
        push(wa.at[y], wa.at[y], 24, at_y((y + j) % ny))

    pending.append((wa.at[0 : ny - 1], 24))

    slot_at = iota((rows, 1), 0).astype(F32)

    def scatter(r0, r1):
        @pl.loop(0, nx)
        def _(view):
            asks = asked_all[view]
            asks = jnp.concatenate([asks[r : r + 1, :] for r in range(r0, r1)], axis=1)
            high, low = split(rows_of(all_f.at[view, r0:r1], (r1 - r0) * strips))
            came = jnp.concatenate([high, low], axis=1)

            @pl.loop(0, prims // rows)
            def _(i):
                start = pl.multiple_of(i * rows, rows)
                here = pl.ds(start, rows)
                hits = jnp.where(slot_at + (i * rows).astype(F32) == asks, 1.0, 0.0).astype(BF16)
                both = mm(hits, came)
                both = both[:, 0:width] + both[:, width:]
                total[here, :] += both

    landed(all_f.at[:, 0:half], 20)
    total[...] = jnp.zeros((prims, width), F32)
    scatter(0, half)

    if ny > 1:
        landed(wa.at[0 : ny - 1], 24)
    wfin[c, z] = rows_of(wa, per_z)

    @pl.loop(1, nz)
    def _(j):
        push(wfin.at[c, z], wfin.at[c, z], 25, (v, y, (z + j) % nz, c))

    if nz > 1:
        pending.append((wfin.at[c, 0 : nz - 1], 25))

    landed(all_f.at[:, half:RANKS], 21)
    scatter(half, RANKS)
    save_f = pltpu.make_async_copy(total, feature_out, local.at[3])
    save_f.start()

    if nz > 1:
        landed(wfin.at[c, 0 : nz - 1], 25)
    push(wfin.at[c], wfin.at[c], 26, other)
    pending.append((wfin.at[c], 26))

    landed(all_g, 22)

    def geometry_of(view):
        pieces = turned(rows_of(all_g.at[view], strips))
        pieces = jnp.concatenate([pieces[8 * r : 8 * r + 8, :] for r in range(RANKS)], axis=1)
        return three(pieces)

    came_g = [geometry_of(view) for view in range(nx)]
    asks_g = [
        jnp.concatenate([asked_all[view][r : r + 1, :] for r in range(RANKS)], axis=1) for view in range(nx)
    ]
    for i in range(prims // rows):
        acc = jnp.zeros((24, rows), F32)
        for view in range(nx):
            hits = jnp.where(slot_at + float(i * rows) == asks_g[view], 1.0, 0.0).astype(BF16)
            acc = acc + mm(came_g[view], hits, 1, 1)
        acc = acc[0:8] + acc[8:16] + acc[16:24]
        geometry_out[:, i * rows : (i + 1) * rows] = acc[0:7]

    landed(wfin.at[0], 26)
    save_w = pltpu.make_async_copy(wfin, weight_out, local.at[4])
    save_w.start()
    for ref, n in pending:
        sent(ref, n)
    save_f.wait()
    save_w.wait()


def per_device(sizes, *arrays):
    means, inv_scales, correlation, opacity, features, cameras, owners, slots, lengths, target, weights, bias = arrays
    nx, ny, nz, nc, entries, prims, height = sizes
    zc = nz * nc
    strips = ny * zc
    width = 128
    pixels = height * 16
    per_z = 9 * width // zc
    per_y = per_z // ny
    vmem = pl.BlockSpec(memory_space=pltpu.VMEM)
    smem = pl.BlockSpec(memory_space=pltpu.SMEM)
    any_ = pl.BlockSpec(memory_space=pl.ANY)

    def f32(*shape):
        return pltpu.VMEM(shape, F32)

    def planes(n):
        return f32(n, zc, ny, 1, width)

    geometry, feature, weight, b_grad = pl.pallas_call(
        functools.partial(kernel, sizes),
        name="splat_step",
        out_shape=(
            jax.ShapeDtypeStruct((7, prims), F32),
            jax.ShapeDtypeStruct((prims, width), F32),
            jax.ShapeDtypeStruct((nc, nz, per_z, width), F32),
            jax.ShapeDtypeStruct((1, width), F32),
        ),
        in_specs=[vmem] * 4 + [smem, vmem, vmem, smem, vmem] + [any_] * 3,
        out_specs=(vmem, any_, any_, vmem),
        scratch_shapes=[
            f32(prims, width), f32(pixels, width), f32(9 * width, width), f32(8, prims),
            pltpu.VMEM((width, prims), BF16), pltpu.VMEM((prims, 2 * width), BF16),
            pltpu.VMEM((9 * width, 2 * width), BF16), pltpu.VMEM((3, 2, width, 3 * width), BF16),
            pltpu.VMEM((RANKS * strips, prims), BF16), f32(2, 16, width),
            planes(1), planes(1), planes(1), f32(nx, 8, strips),
            planes(1), planes(1), planes(1), planes(RANKS), planes(RANKS), planes(RANKS),
            f32(pixels + 64, width), planes(RANKS), planes(RANKS), planes(RANKS), planes(1), planes(1), planes(1),
            f32(nx, RANKS, zc, ny, 1, width), f32(nx, 1, zc, ny, 1, width),
            f32(prims, width), f32(9 * width, width), f32(nc, nz, per_z + 8, width), f32(nz, per_z + 8, width),
            f32(nz, per_z + 8, width), f32(nz, per_z + 8, width),
            f32(ny, per_y + 1, 1, width), f32(ny, per_y + 1, 1, width), f32(per_y + 1, 1, width),
            f32(nx, per_y + 1, 1, width), f32(ny, per_y, 1, width), f32(nc, nz, per_z, width),
            pltpu.SemaphoreType.DMA((27,)), pltpu.SemaphoreType.DMA((27,)), pltpu.SemaphoreType.DMA((5,)),
        ],
        compiler_params=pltpu.CompilerParams(
            collective_id=0, has_side_effects=True, vmem_limit_bytes=56 * 1024 * 1024
        ),
    )(
        means, inv_scales, correlation.reshape(1, prims), opacity.reshape(1, prims), cameras.reshape(1, 8),
        owners.reshape(1, entries), slots.reshape(1, entries), lengths.reshape(1, 1), bias.reshape(1, width),
        features, target.reshape(pixels, width), weights.reshape(9 * width, width),
    )
    return geometry, feature, weight.reshape(3, 3, width, width), b_grad.reshape(width)


def built(mesh, ny, nz, nc, entries, prims, height):
    nx = mesh.shape["view"]
    finer = Mesh(mesh.devices.reshape(nx, ny, nz, nc), ("view",) + STRIP)
    return jax.shard_map(
        functools.partial(per_device, (nx, ny, nz, nc, entries, prims, height)),
        mesh=finer,
        in_specs=(
            P(None, STRIP),
            P(None, STRIP),
            P(STRIP),
            P(STRIP),
            P(STRIP, None),
            P("view", None, None),
            P("view", STRIP, None, None),
            P("view", STRIP, None),
            P("view", STRIP),
            P("view", STRIP, None, None),
            P(),
            P(),
        ),
        out_specs=(P(None, STRIP), P(STRIP, None), P(), P()),
        check_vma=False,
    )


def solution(mesh):
    return built(mesh, 8, 8, 2, 256, 2048, 16)
```

```python
import functools

import jax
import jax.numpy as jnp
from jax import lax
from jax.experimental import pallas as pl
from jax.experimental.pallas import tpu as pltpu
from jax.sharding import Mesh
from jax.sharding import PartitionSpec as P

STRIP = ("strip_0", "strip_1", "strip_2")
MESH = pl.DeviceIdType.MESH
F32 = jnp.float32
BF16 = jnp.bfloat16
VMEM_LIMIT = 24 * 1024 * 1024
RANKS = 4


def iota(shape, dim):
    return lax.broadcasted_iota(jnp.int32, shape, dim)


def mm(a, b, ca=1, cb=0):
    return lax.dot_general(a, b, (((ca,), (cb,)), ((), ())), preferred_element_type=F32)


def split(x):
    high = x.astype(BF16)
    return high, (x - high.astype(F32)).astype(BF16)


def split3(x):
    high = x.astype(BF16)
    rest = x - high.astype(F32)
    mid = rest.astype(BF16)
    return high, mid, (rest - mid.astype(F32)).astype(BF16)


def rows_of(ref, n):
    return ref.reshape(n, ref.shape[-1])[...]


def fill(ref, value):
    ref.reshape(*value.shape)[...] = value


def kernel(
    sizes,
    means, inv_scales, correlation, opacity, cameras, owners_hbm, slots_hbm, lengths, bias_hbm,
    features_hbm, target_hbm, weights_hbm,
    geometry_out, feature_out, weight_out, bias_out,
    owners, slots, bias, feat, targ, wts, table, g_parts, f_parts, w_parts, w_turned, onehot, halo_t,
    req, req_mid, req_got, asked_all,
    geo, geo_mid, geo_got, fea, fea_mid, fea_got,
    image, back, back_mid, back_got, bgeo, bgeo_mid, bgeo_got, all_f, all_g,
    total, total_g, wl, wx, wc, wa, wa_got, wb, wb_got, wa2, wa2_got, wb2, wb2_got, wq, wq_got, wa3, wb3, wfin,
    send, recv, local,
):
    nx, ny, nz, nc, entries, prims, height = sizes
    zc_count = nz * nc
    strips = ny * zc_count
    places = RANKS * strips
    width = 128
    pixels = height * 16
    extended = pixels + 32
    v = lax.axis_index("view")
    y = lax.axis_index("strip_0")
    z = lax.axis_index("strip_1")
    c = lax.axis_index("strip_2")
    zc = z * nc + c
    strip = y * zc_count + zc

    def at_zc(k):
        return (v, y, k // nc, k % nc)

    def at_y(k):
        return (v, k, z, c)

    def at_x(k):
        return (k, y, z, c)

    def at_strip(k):
        return (v, k // zc_count, (k % zc_count) // nc, k % nc)

    up = at_strip((strip + strips - 1) % strips)
    down = at_strip((strip + 1) % strips)

    def push(src, dst, n, device):
        pltpu.make_async_remote_copy(
            src_ref=src, dst_ref=dst, send_sem=send.at[n], recv_sem=recv.at[n],
            device_id=device, device_id_type=MESH,
        ).start()

    def keep(src, dst, n):
        pltpu.make_async_copy(src, dst, recv.at[n]).start()

    def landed(ref, n):
        pltpu.make_async_copy(ref, ref, recv.at[n]).wait()

    def sent(ref, n):
        pltpu.make_async_copy(ref, ref, send.at[n]).wait()

    pending = []

    def drain():
        for ref, n in pending:
            sent(ref, n)
        pending.clear()

    def to_zc(src, dst, n):
        for j in range(1, zc_count):
            k = (zc + j) % zc_count
            push(src.at[:, k], dst.at[:, zc], n, at_zc(k))

        keep(src.at[:, zc], dst.at[:, zc], n)
        if zc_count > 1:
            pending.append((src.at[:, 0 : zc_count - 1], n))

    def to_y(src, dst, n):
        for j in range(1, ny):
            k = (y + j) % ny
            push(src.at[:, :, k], dst.at[:, :, y], n, at_y(k))

        keep(src.at[:, :, y], dst.at[:, :, y], n)
        if ny > 1:
            pending.append((src.at[:, :, 0 : ny - 1], n))

    load_o = pltpu.make_async_copy(owners_hbm, owners, local.at[5])
    load_s = pltpu.make_async_copy(slots_hbm, slots, local.at[6])
    load_b = pltpu.make_async_copy(bias_hbm, bias, local.at[7])
    load_g = [
        pltpu.make_async_copy(ref, table.at[a:b], local.at[8 + i])
        for i, (ref, a, b) in enumerate(
            ((means, 0, 3), (inv_scales, 3, 5), (correlation, 5, 6), (opacity, 6, 7))
        )
    ]
    load_o.start()
    load_s.start()
    load_f = pltpu.make_async_copy(features_hbm, feat, local.at[0])
    load_t = pltpu.make_async_copy(target_hbm, targ, local.at[1])
    load_w = pltpu.make_async_copy(weights_hbm, wts, local.at[2])

    barrier = pltpu.get_barrier_semaphore()

    for j in range(1, zc_count):
        pl.semaphore_signal(barrier, inc=1, device_id=at_zc((zc + j) % zc_count), device_id_type=MESH)

    for j in range(1, ny):
        pl.semaphore_signal(barrier, inc=1, device_id=at_y((y + j) % ny), device_id_type=MESH)

    for j in range(1, nx):
        pl.semaphore_signal(barrier, inc=1, device_id=at_x((v + j) % nx), device_id_type=MESH)

    pl.semaphore_signal(barrier, inc=1, device_id=up, device_id_type=MESH)
    pl.semaphore_signal(barrier, inc=1, device_id=down, device_id_type=MESH)

    for load in load_g + [load_f, load_t, load_w, load_b]:
        load.start()

    def column(row):
        n = row.shape[1]
        same = iota((n, n), 0) == iota((n, n), 1)
        return jnp.sum(jnp.where(same, jnp.broadcast_to(row, (n, n)), 0.0), axis=1, keepdims=True)

    first = iota((entries, entries), 0)
    second = iota((entries, entries), 1)
    load_o.wait()
    owner = owners[...]
    home = ((owner % zc_count) * ny + owner // zc_count).astype(F32)
    home_col = column(home)
    alike = home_col == home
    rank_row = jnp.sum(jnp.where(alike & (first < second), 1.0, 0.0), axis=0, keepdims=True)
    at_home = jnp.where(iota((strips, entries), 0).astype(F32) == home, 1.0, 0.0).astype(BF16)
    load_s.wait()
    slot = slots[...].astype(F32)
    slot_high = jnp.floor(slot * (1.0 / 64.0))
    slot_low = slot - 64.0 * slot_high
    row_at = iota((width, entries), 0).astype(F32)
    sought = jnp.where(row_at == rank_row, slot_high, 0.0) + jnp.where(row_at - 8.0 == rank_row, slot_low, 0.0)
    sought = mm(at_home, sought.astype(BF16), 1, 1)
    fill(req, sought * 64.0 + pltpu.roll(sought, width - 8, 1))

    pl.semaphore_wait(barrier, zc_count + ny + nx - 3 + 2)

    to_zc(req, req_mid, 0)
    push(target_hbm.at[0:16], halo_t.at[1], 1, up)
    push(target_hbm.at[pixels - 16 : pixels], halo_t.at[0], 1, down)
    pending.append((halo_t, 1))

    for load in load_g:
        load.wait()
    whole = jnp.concatenate([table[...], jnp.zeros((1, prims), F32)], axis=0)
    g_high, g_mid, g_low = (part.astype(F32) for part in split3(whole))
    g_parts[...] = jnp.concatenate(
        [g_high] * RANKS + [g_mid] * RANKS + [g_low] * RANKS + [jnp.zeros((32, prims), F32)], axis=0
    ).astype(BF16)
    load_f.wait()
    rows = min(prims, 512)

    @pl.loop(0, prims // rows)
    def _(i):
        here = pl.ds(pl.multiple_of(i * rows, rows), rows)
        high, low = split(feat[here, :])
        f_parts[here, 0:width] = high
        f_parts[here, width : 2 * width] = low

    landed(req_mid, 0)
    to_y(req_mid, req_got, 2)

    load_w.wait()
    for tap in range(9):
        high, low = split(wts[tap * width : (tap + 1) * width, :])
        w_parts[tap * width : (tap + 1) * width, 0:width] = high
        w_parts[tap * width : (tap + 1) * width, width : 2 * width] = low
        a, b = 2 - tap // 3, 2 - tap % 3
        w_turned[a, 0, :, b * width : (b + 1) * width] = high
        w_turned[a, 1, :, b * width : (b + 1) * width] = low
    load_t.wait()
    load_b.wait()
    rank_col = jnp.sum(jnp.where(alike & (second < first), 1.0, 0.0), axis=1, keepdims=True)
    place_row = rank_row * float(strips) + home
    place_col = rank_col * float(strips) + home_col
    to_place = jnp.where(iota((places, entries), 0).astype(F32) == place_row, 1.0, 0.0).astype(BF16)
    from_place = jnp.where(iota((entries, places), 1).astype(F32) == place_col, 1.0, 0.0).astype(BF16)
    before = jnp.where(first < second, 1.0, 0.0).astype(BF16)
    behind = jnp.where(first > second, 1.0, 0.0).astype(BF16)

    landed(req_got, 2)
    asked = rows_of(req_got, strips)
    square = jnp.concatenate([asked, jnp.zeros((width - strips, width), F32)], axis=0) if strips < width else asked
    asked_rows = jnp.transpose(square)[0:8, 0:strips]
    asked_all[v] = asked_rows

    for j in range(1, nx):
        push(asked_all.at[v], asked_all.at[v], 3, at_x((v + j) % nx))

    if nx > 1:
        pending.append((asked_all.at[0 : nx - 1], 3))

    block = min(prims, 256)
    ident = iota((1, block), 1).astype(F32).astype(BF16)
    packed = jnp.zeros((strips, width), F32)
    lanes = iota((strips, width), 1)
    for r in range(RANKS):
        for k in range(prims // block):
            near = (asked[:, r : r + 1] - float(k * block)).astype(BF16)
            onehot[r * strips : (r + 1) * strips, k * block : (k + 1) * block] = jnp.where(
                ident == near, jnp.ones((), BF16), jnp.zeros((), BF16)
            )
    for r in range(RANKS):
        found = mm(onehot[r * strips : (r + 1) * strips, :], g_parts[...], 1, 1)
        packed = packed + jnp.where((lanes % 32) // 8 == r, found, 0.0)

    def folded(x):
        x = x + pltpu.roll(x, width - 32, 1) + pltpu.roll(x, width - 64, 1)
        return jnp.where(lanes < 32, x, 0.0)

    fill(geo, folded(packed))
    to_zc(geo, geo_mid, 4)

    for r in range(RANKS):
        found = mm(onehot[r * strips : (r + 1) * strips, :], f_parts[...])
        fill(fea.at[r], found[:, 0:width] + found[:, width : 2 * width])
        one = slice(r, r + 1)
        (to_y if r % 2 else to_zc)(fea.at[one], fea_mid.at[one], 37 + r)
    landed(geo_mid, 4)
    to_y(geo_mid, geo_got, 7)
    for r in range(RANKS):
        one = slice(r, r + 1)
        landed(fea_mid.at[one], 37 + r)
        (to_zc if r % 2 else to_y)(fea_mid.at[one], fea_got.at[one], 41 + r)

    landed(geo_got, 7)

    def turned(x):
        x = jnp.concatenate([x, jnp.zeros((width - strips, width), F32)], axis=0) if strips < width else x
        return jnp.transpose(x)[0 : 8 * RANKS, 0:strips]

    def three(x):
        return jnp.concatenate([part.astype(F32) for part in split3(x)], axis=0).astype(BF16)

    spread = mm(three(turned(rows_of(geo_got, strips))), at_home)
    n8 = 8 * RANKS
    spread = spread[0:n8] + spread[n8 : 2 * n8] + spread[2 * n8 : 3 * n8]
    g = jnp.zeros((8, entries), F32)
    for r in range(RANKS):
        g = g + jnp.where(rank_row == float(r), spread[8 * r : 8 * r + 8, :], 0.0)

    def cam(axis, k):
        return cameras[0, axis, k]

    def center(axis):
        return 8.0 + 4.0 * (
            cam(axis, 0) * g[0:1] + cam(axis, 1) * g[1:2] + cam(axis, 2) * g[2:3] + cam(axis, 3)
        )

    pixel = iota((pixels, 1), 0)
    across = (pixel % 16).astype(F32) + 0.5
    downward = (pixel // 16).astype(F32) + 0.5
    du = across - center(0)
    dv = downward - center(1)
    a = g[3:4] * du
    b = g[4:5] * dv
    skew = g[5:6]
    grown = jnp.exp(-0.5 * (a * a + 2.0 * skew * a * b + b * b))
    solid = 1.0 / (1.0 + jnp.exp(-g[6:7]))
    raw = solid * grown
    alive = jnp.where(iota((1, entries), 1) < lengths[0, 0], 1.0, 0.0)
    cover = jnp.minimum(raw, 0.99) * alive
    fades = jnp.log(1.0 - cover)
    f_high, f_mid, f_low = split3(fades)
    through = jnp.exp(mm(f_high, before) + mm(f_mid, before) + mm(f_low, before))
    weight = cover * through
    weight_high, weight_low = split(weight)

    weight_t_high = jnp.transpose(weight_high.astype(F32)).astype(BF16)
    weight_t_low = jnp.transpose(weight_low.astype(F32)).astype(BF16)
    for r in range(RANKS):
        landed(fea_got.at[r : r + 1], 41 + r)
    high, low = split(rows_of(fea_got, places))
    listed = mm(from_place, jnp.concatenate([high, low], axis=1)).astype(BF16)
    both = mm(weight_high, listed)
    tile = both[:, 0:width] + both[:, width:] + mm(weight_low, listed[:, 0:width])
    image[32 : 32 + pixels, :] = tile

    push(image.at[32:64], image.at[32 + pixels : 64 + pixels], 10, up)
    push(image.at[pixels : 32 + pixels], image.at[0:32], 10, down)
    pending.append((image.at[0:64], 10))

    def sideways(x):
        n = x.shape[0]
        col = iota((n, 1), 0) % 16
        left = jnp.where(col == 0, 0.0, pltpu.roll(x, 1, 0))
        right = jnp.where(col == 15, 0.0, pltpu.roll(x, n - 1, 0))
        return split(jnp.concatenate([left, x, right], axis=1))

    def taps(i):
        return w_parts[i * 3 * width : (i + 1) * 3 * width, :]

    def product(high, low, part):
        both = mm(high, part)
        return both[:, 0:width] + (both[:, width:] + mm(low, part[:, 0:width]))

    edge = jnp.zeros((32, width), F32)
    pic_high, pic_low = sideways(jnp.concatenate([edge, tile, edge], axis=0))
    decoded = jnp.zeros((extended, width), F32)
    for i in range(3):
        here = slice(i * 16, i * 16 + extended)
        decoded = decoded + product(pic_high[here, :], pic_low[here, :], taps(i))
    decoded = decoded + bias[...]
    pic_t_high = jnp.transpose(pic_high.astype(F32)).astype(BF16)
    pic_t_low = jnp.transpose(pic_low.astype(F32)).astype(BF16)
    drain()
    landed(halo_t, 1)
    aim = jnp.concatenate([halo_t[0], targ[...], halo_t[1]], axis=0)
    decoded = decoded - aim

    landed(image.at[0:64], 10)
    has_up = strip > 0
    has_down = strip < strips - 1
    beyond = jnp.concatenate([image[0:32, :], image[32 + pixels :, :]], axis=0)
    known = jnp.where(iota((64, 1), 0) < 32, has_up.astype(F32), has_down.astype(F32)) > 0.5
    out_high, out_low = sideways(jnp.where(known, beyond, 0.0))
    top = product(out_high[0:32, :], out_low[0:32, :], taps(0))
    mid = product(out_high[16:48, :], out_low[16:48, :], taps(1))
    low = product(out_high[32:64, :], out_low[32:64, :], taps(2))
    decoded = jnp.concatenate(
        [
            decoded[0:16] + (top[0:16] + mid[0:16]),
            decoded[16:32] + top[16:32],
            decoded[32 : extended - 32],
            decoded[extended - 32 : extended - 16] + low[0:16],
            decoded[extended - 16 :] + (low[16:32] + mid[16:32]),
        ],
        axis=0,
    )
    rows_at = iota((extended, 1), 0)
    inside = ((rows_at >= 16) | has_up) & ((rows_at < 16 + pixels) | has_down)
    residual = jnp.where(inside, decoded, 0.0)
    res_high, res_low = sideways(residual)
    grad = jnp.zeros((pixels, width), F32)
    for i in range(3):
        here = slice(i * 16, i * 16 + pixels)
        grad = grad + (
            mm(res_high[here, :], w_turned[i, 0], 1, 1)
            + (mm(res_high[here, :], w_turned[i, 1], 1, 1) + mm(res_low[here, :], w_turned[i, 0], 1, 1))
        )
    grad_high, grad_low = split(grad)

    both = mm(weight_t_high, jnp.concatenate([grad_high, grad_low], axis=1))
    f_grad = both[:, 0:width] + (both[:, width:] + mm(weight_t_low, grad_high))
    high, low = split(f_grad)
    f_grad = jnp.concatenate([high, low], axis=1)
    for r in range(RANKS):
        both = mm(to_place[r * strips : (r + 1) * strips, :], f_grad)
        fill(back.at[r], both[:, 0:width] + both[:, width:])
        one = slice(r, r + 1)
        (to_y if r % 2 else to_zc)(back.at[one], back_mid.at[one], 11 + r)

    own = residual[16 : 16 + pixels, :]
    shifted = []
    for i in range(3):
        shifted.append(
            jnp.concatenate(
                [jnp.zeros(((i + 1) * 16, width), F32), own, jnp.zeros((64 - (i + 1) * 16, width), F32)], axis=0
            )
        )
    own_high, own_low = split(jnp.concatenate(shifted, axis=1))
    w_grad = mm(pic_t_high, own_high) + (mm(pic_t_high, own_low) + mm(pic_t_low, own_high))
    next_high = jnp.concatenate([own_high[16:32], own_high[pixels + 32 : pixels + 48]], axis=0)
    next_low = jnp.concatenate([own_low[16:32], own_low[pixels + 32 : pixels + 48]], axis=0)
    near_high, near_low = out_high[16:48], out_low[16:48]
    w_grad = w_grad + (mm(near_high, next_high, 0, 0) + (mm(near_high, next_low, 0, 0) + mm(near_low, next_high, 0, 0)))
    for i in range(3):
        wl[i * 3 * width : (i + 1) * 3 * width, :] = w_grad[:, i * width : (i + 1) * width]
    b_grad = jnp.broadcast_to(jnp.sum(own, axis=0, keepdims=True), (8, width))
    rows_a, rows_b, pa, pb, ra, rb = decoder_rows(sizes)
    core_rows = rows_a + rows_b
    for k in range(nc):
        base = k * core_rows
        wx[k, 0:rows_a, :] = wl[base : base + rows_a, :]
        for i in range(ny):
            at = rows_a + i * (pb + 8)
            wx[k, at : at + pb, :] = wl[base + rows_a + i * pb : base + rows_a + (i + 1) * pb, :]
            wx[k, at + pb : at + pb + 8, :] = b_grad
    other = (v, y, z, 1 - c)
    push(wx.at[1 - c], wc, 15, other)
    pending.append((wc, 15))

    d_weight = mm(jnp.concatenate([grad_high, grad_high], axis=1), listed, 1, 1) + mm(
        grad_low, listed[:, 0:width], 1, 1
    )
    f_high, f_mid, f_low = split3(d_weight * weight)
    later = mm(f_high, behind) + mm(f_mid, behind) + mm(f_low, behind)
    d_cover = d_weight * through - later / (1.0 - cover)
    d_raw = jnp.where(raw < 0.99, d_cover, 0.0) * alive
    d_grown = d_raw * raw
    u = (a + skew * b) * d_grown
    w = (b + skew * a) * d_grown

    def summed(x):
        return jnp.sum(x, axis=0, keepdims=True)

    d_col = 4.0 * g[3:4] * summed(u)
    d_row = 4.0 * g[4:5] * summed(w)
    parts = [cam(0, k) * d_col + cam(1, k) * d_row for k in range(3)]
    parts += [-summed(u * du), -summed(w * dv), -summed(d_grown * a * b), summed(d_grown) * (1.0 - solid)]
    parts.append(jnp.zeros((1, entries), F32))
    g_grad = jnp.concatenate(parts, axis=0)
    by_rank = jnp.concatenate([jnp.where(rank_row == float(r), g_grad, 0.0) for r in range(RANKS)], axis=0)
    by_rank = jnp.concatenate([part.astype(F32) for part in split3(by_rank)] + [jnp.zeros((32, entries), F32)], axis=0)
    fill(bgeo, folded(mm(at_home, by_rank.astype(BF16), 1, 1)))
    to_zc(bgeo, bgeo_mid, 16)

    landed(wc, 15)
    wa[...] = (wx[c, 0:rows_a, :] + wc[0:rows_a, :]).reshape(nz, pa, width)
    wb[...] = (wx[c, rows_a:, :] + wc[rows_a:, :]).reshape(ny, pb + 8, width)

    def along_z(src, dst, n):
        for j in range(1, nz):
            k = (z + j) % nz
            push(src(k), dst(z), n, (v, y, k, c))

    def along_y(src, dst, n):
        for j in range(1, ny):
            k = (y + j) % ny
            push(src(k), dst(y), n, at_y(k))

    def added(ref, n):
        sums = ref[0]
        for k in range(1, n):
            sums = sums + ref[k]
        return sums

    along_z(lambda k: wa.at[k], lambda k: wa_got.at[k], 17)
    keep(wa.at[z], wa_got.at[z], 17)
    along_y(lambda k: wb.at[k], lambda k: wb_got.at[k], 18)
    keep(wb.at[y], wb_got.at[y], 18)
    if nz > 1:
        pending.append((wa.at[0 : nz - 1], 17))
    if ny > 1:
        pending.append((wb.at[0 : ny - 1], 18))

    for r in range(RANKS):
        one = slice(r, r + 1)
        landed(back_mid.at[one], 11 + r)
        (to_zc if r % 2 else to_y)(back_mid.at[one], back_got.at[one], 19 + r)
    landed(bgeo_mid, 16)
    to_y(bgeo_mid, bgeo_got, 23)

    landed(wa_got, 17)
    sums = added(wa_got, nz)
    for k in range(ny):
        fill(wa2.at[k], sums[k * ra : (k + 1) * ra, :])
    along_y(lambda k: wa2.at[k], lambda k: wa2_got.at[k], 24)
    keep(wa2.at[y], wa2_got.at[y], 24)
    landed(wb_got, 18)
    sums = added(wb_got, ny)
    for k in range(nz):
        fill(wb2.at[k, 0:rb], sums[k * rb : (k + 1) * rb, :])
        fill(wb2.at[k, rb : rb + 1], sums[pb : pb + 1, :])
    along_z(lambda k: wb2.at[k], lambda k: wb2_got.at[k], 25)
    keep(wb2.at[z], wb2_got.at[z], 25)
    if ny > 1:
        pending.append((wa2.at[0 : ny - 1], 24))
    if nz > 1:
        pending.append((wb2.at[0 : nz - 1], 25))

    def to_x(src, dst, n):
        for j in range(1, nx):
            push(src, dst, n, at_x((v + j) % nx))

        keep(src, dst, n)
        for _ in range(nx - 1):
            pending.append((src, n))

    def plane(r):
        return all_f.at[v, r]

    drain()
    landed(back_got.at[0:1], 19)
    to_x(back_got.at[0], plane(0), 26)
    landed(bgeo_got, 23)
    to_x(bgeo_got.at[0], all_g.at[v, 0], 30)

    landed(wa2_got, 24)
    landed(wb2_got, 25)
    wq[0:ra] = added(wa2_got, ny)
    wq[ra:] = added(wb2_got, nz)
    to_x(wq, wq_got.at[v], 31)
    for r in range(1, RANKS):
        landed(back_got.at[r : r + 1], 19 + r)
        to_x(back_got.at[r], plane(r), 26 + r)

    if nx > 1:
        landed(asked_all.at[0 : nx - 1], 3)
    slot_at = iota((block, 1), 0).astype(F32).astype(BF16)

    def geometry_of(r):
        return three(jnp.concatenate([shared_g[k][8 * r : 8 * r + 8, :] for k in range(nx)], axis=1))

    def scatter(r):
        asks = jnp.concatenate([asked_all[k][r : r + 1, :] for k in range(nx)], axis=1)
        came_g = geometry_of(r)
        high, low = split(jnp.concatenate([rows_of(all_f.at[k, r], strips) for k in range(nx)], axis=0))
        came = jnp.concatenate([high, low], axis=1)

        @pl.loop(0, prims // rows)
        def _(i):
            here = pl.ds(pl.multiple_of(i * rows, rows), rows)
            base = (i * rows).astype(F32)
            hits = jnp.concatenate(
                [
                    jnp.where(
                        slot_at == (asks - (base + float(k * block))).astype(BF16),
                        jnp.ones((), BF16),
                        jnp.zeros((), BF16),
                    )
                    for k in range(rows // block)
                ],
                axis=0,
            )
            both = mm(hits, came)
            both = both[:, 0:width] + both[:, width:]
            found = mm(came_g, hits, 1, 1)
            found = found[0:8] + found[8:16] + found[16:24]
            if r:
                total[here, :] += both
                total_g[i] += found
            else:
                total[here, :] = both
                total_g[i] = found

    landed(wq_got, 31)
    sums = added(wq_got, nx)
    bias_out[...] = sums[ra + rb]
    wa3[y] = sums[0:ra]
    wb3[z] = sums[ra : ra + rb]
    along_y(lambda k: wa3.at[y], lambda k: wa3.at[k], 32)
    along_z(lambda k: wb3.at[z], lambda k: wb3.at[k], 33)
    if ny > 1:
        pending.append((wa3.at[0 : ny - 1], 32))
    if nz > 1:
        pending.append((wb3.at[0 : nz - 1], 33))

    landed(all_g.at[:, 0], 30)
    shared_g = [turned(rows_of(all_g.at[k], strips)) for k in range(nx)]
    landed(all_f.at[:, 0], 26)
    scatter(0)

    landed(all_f.at[:, 1], 27)
    scatter(1)

    if ny > 1:
        landed(wa3.at[0 : ny - 1], 32)
    if nz > 1:
        landed(wb3.at[0 : nz - 1], 33)

    def part_a(k):
        return wfin.at[c, pl.ds(pl.multiple_of(k * pa, 8), pa)]

    def part_b(k):
        return wfin.at[c, pl.ds(pl.multiple_of(rows_a + k * pb, 8), pb)]

    wfin[c, pl.ds(pl.multiple_of(z * pa, 8), pa), :] = rows_of(wa3, pa)
    wfin[c, pl.ds(pl.multiple_of(rows_a + y * pb, 8), pb), :] = rows_of(wb3, pb)
    along_z(lambda k: part_a(z), part_a, 34)
    along_y(lambda k: part_b(y), part_b, 35)
    gone_a = wfin.at[0, 0 : (nz - 1) * pa]
    gone_b = wfin.at[0, 0 : (ny - 1) * pb]
    if nz > 1:
        pending.append((gone_a, 34))
    if ny > 1:
        pending.append((gone_b, 35))

    landed(all_f.at[:, 2], 28)
    scatter(2)
    landed(all_f.at[:, 3], 29)
    scatter(3)
    save_f = pltpu.make_async_copy(total, feature_out, local.at[3])
    save_f.start()
    for i in range(prims // rows):
        geometry_out[:, i * rows : (i + 1) * rows] = total_g[i][0:7]

    if nz > 1:
        landed(gone_a, 34)
    if ny > 1:
        landed(gone_b, 35)
    push(wfin.at[c], wfin.at[c], 36, other)
    pending.append((wfin.at[0], 36))
    landed(wfin.at[0], 36)
    save_w = pltpu.make_async_copy(wfin, weight_out, local.at[4])
    save_w.start()
    drain()
    save_f.wait()
    save_w.wait()


def decoder_rows(sizes):
    nx, ny, nz, nc, entries, prims, height = sizes
    rows = 9 * 128 // nc
    rows_a = rows * 5 // 9
    rows_b = rows - rows_a
    return rows_a, rows_b, rows_a // nz, rows_b // ny, rows_a // nz // ny, rows_b // nz // ny


def per_device(sizes, *arrays):
    means, inv_scales, correlation, opacity, features, cameras, owners, slots, lengths, target, weights, bias = arrays
    nx, ny, nz, nc, entries, prims, height = sizes
    zc = nz * nc
    strips = ny * zc
    width = 128
    pixels = height * 16
    rows = min(prims, 512)
    rows_a, rows_b, pa, pb, ra, rb = decoder_rows(sizes)
    vmem = pl.BlockSpec(memory_space=pltpu.VMEM)
    smem = pl.BlockSpec(memory_space=pltpu.SMEM)
    any_ = pl.BlockSpec(memory_space=pl.ANY)
    hbm = pl.BlockSpec(memory_space=pltpu.HBM)

    def f32(*shape):
        return pltpu.VMEM(shape, F32)

    def planes(n):
        return f32(n, zc, ny, 1, width)

    geometry, feature, weight, b_grad = pl.pallas_call(
        functools.partial(kernel, sizes),
        name="splat_step",
        out_shape=(
            jax.ShapeDtypeStruct((7, prims), F32),
            jax.ShapeDtypeStruct((prims, width), F32),
            jax.ShapeDtypeStruct((nc, rows_a + rows_b, width), F32),
            jax.ShapeDtypeStruct((1, width), F32),
        ),
        in_specs=[hbm] * 4 + [smem, hbm, hbm, smem, hbm] + [hbm] * 3,
        out_specs=(vmem, any_, any_, vmem),
        scratch_shapes=[
            pltpu.VMEM((1, entries), jnp.int32), pltpu.VMEM((1, entries), jnp.int32), f32(1, width),
            f32(prims, width), f32(pixels, width), f32(9 * width, width), f32(7, prims),
            pltpu.VMEM((width, prims), BF16), pltpu.VMEM((prims, 2 * width), BF16),
            pltpu.VMEM((9 * width, 2 * width), BF16), pltpu.VMEM((3, 2, width, 3 * width), BF16),
            pltpu.VMEM((RANKS * strips, prims), BF16), f32(2, 16, width),
            planes(1), planes(1), planes(1), f32(nx, 8, strips),
            planes(1), planes(1), planes(1), planes(RANKS), planes(RANKS), planes(RANKS),
            f32(pixels + 64, width), planes(RANKS), planes(RANKS), planes(RANKS), planes(1), planes(1), planes(1),
            f32(nx, RANKS, zc, ny, 1, width), f32(nx, 1, zc, ny, 1, width),
            f32(prims, width), f32(prims // rows, 8, rows), f32(9 * width, width),
            f32(nc, rows_a + rows_b + 8 * ny, width), f32(rows_a + rows_b + 8 * ny, width),
            f32(nz, pa, width), f32(nz, pa, width), f32(ny, pb + 8, width), f32(ny, pb + 8, width),
            f32(ny, ra, 1, width), f32(ny, ra, 1, width), f32(nz, rb + 1, 1, width), f32(nz, rb + 1, 1, width),
            f32(ra + rb + 1, 1, width), f32(nx, ra + rb + 1, 1, width),
            f32(ny, ra, 1, width), f32(nz, rb, 1, width), f32(nc, rows_a + rows_b, width),
            pltpu.SemaphoreType.DMA((45,)), pltpu.SemaphoreType.DMA((45,)), pltpu.SemaphoreType.DMA((12,)),
        ],
        compiler_params=pltpu.CompilerParams(
            collective_id=0, has_side_effects=True, vmem_limit_bytes=VMEM_LIMIT
        ),
    )(
        *[a if n == 7 else pltpu.with_memory_space_constraint(a, pltpu.HBM) for n, a in enumerate((
        means, inv_scales, correlation.reshape(1, prims), opacity.reshape(1, prims), cameras,
        owners.reshape(1, entries), slots.reshape(1, entries), lengths.reshape(1, 1), bias.reshape(1, width),
        features, target.reshape(pixels, width), weights.reshape(9 * width, width),
        ))],
    )
    return geometry, feature, weight.reshape(3, 3, width, width), b_grad.reshape(width)


def built(mesh, ny, nz, nc, entries, prims, height):
    nx = mesh.shape["view"]
    finer = Mesh(mesh.devices.reshape(nx, ny, nz, nc), ("view",) + STRIP)
    return jax.shard_map(
        functools.partial(per_device, (nx, ny, nz, nc, entries, prims, height)),
        mesh=finer,
        in_specs=(
            P(None, STRIP),
            P(None, STRIP),
            P(STRIP),
            P(STRIP),
            P(STRIP, None),
            P("view", None, None),
            P("view", STRIP, None, None),
            P("view", STRIP, None),
            P("view", STRIP),
            P("view", STRIP, None, None),
            P(),
            P(),
        ),
        out_specs=(P(None, STRIP), P(STRIP, None), P(), P()),
        check_vma=False,
    )


def solution(mesh):
    return built(mesh, 8, 8, 2, 256, 2048, 16)
```

```python
import functools

import jax
import jax.numpy as jnp
from jax import lax
from jax.experimental import pallas as pl
from jax.experimental.pallas import tpu as pltpu
from jax.sharding import Mesh
from jax.sharding import PartitionSpec as P

STRIP = ("strip_0", "strip_1", "strip_2")
MESH = pl.DeviceIdType.MESH
F32 = jnp.float32
BF16 = jnp.bfloat16
VMEM_LIMIT = 24 * 1024 * 1024
RANKS = 4


def iota(shape, dim):
    return lax.broadcasted_iota(jnp.int32, shape, dim)


def mm(a, b, ca=1, cb=0):
    return lax.dot_general(a, b, (((ca,), (cb,)), ((), ())), preferred_element_type=F32)


def split(x):
    high = x.astype(BF16)
    return high, (x - high.astype(F32)).astype(BF16)


def split3(x):
    high = x.astype(BF16)
    rest = x - high.astype(F32)
    mid = rest.astype(BF16)
    return high, mid, (rest - mid.astype(F32)).astype(BF16)


def far_first(n):
    return sorted(range(1, n), key=lambda j: -min(j, n - j))


def rows_of(ref, n):
    return ref.reshape(n, ref.shape[-1])[...]


def fill(ref, value):
    ref.reshape(*value.shape)[...] = value


def kernel(
    sizes,
    means, inv_scales, correlation, opacity, cameras, owners_hbm, slots_hbm, lengths, bias_hbm,
    features_hbm, target_hbm, weights_hbm,
    geometry_out, feature_out, weight_out, bias_out,
    owners, slots, bias, feat, targ, wts, table, g_parts, f_parts, w_parts, w_turned, onehot, halo_t,
    req, req_mid, req_got, asked_all,
    geo, geo_mid, geo_got, fea, fea_mid, fea_got,
    image, back, back_mid, back_got, bgeo, bgeo_mid, bgeo_got, all_f, all_g, own_g,
    total, total_g, wl, wx, wc, wa, wa_got, wb, wb_got, wa2, wa2_got, wb2, wb2_got, wq, wq_got, wa3, wb3, mine_a, mine_b, g_total, b_total,
    send, recv, local,
):
    nx, ny, nz, nc, entries, prims, height = sizes
    zc_count = nz * nc
    strips = ny * zc_count
    places = RANKS * strips
    width = 128
    pixels = height * 16
    extended = pixels + 32
    v = lax.axis_index("view")
    y = lax.axis_index("strip_0")
    z = lax.axis_index("strip_1")
    c = lax.axis_index("strip_2")
    zc = z * nc + c
    strip = y * zc_count + zc

    def at_zc(k):
        return (v, y, k // nc, k % nc)

    def at_y(k):
        return (v, k, z, c)

    def at_x(k):
        return (k, y, z, c)

    def at_strip(k):
        return (v, k // zc_count, (k % zc_count) // nc, k % nc)

    up = at_strip((strip + strips - 1) % strips)
    down = at_strip((strip + 1) % strips)

    def push(src, dst, n, device):
        pltpu.make_async_remote_copy(
            src_ref=src, dst_ref=dst, send_sem=send.at[n], recv_sem=recv.at[n],
            device_id=device, device_id_type=MESH,
        ).start()

    def keep(src, dst, n):
        pltpu.make_async_copy(src, dst, recv.at[n]).start()

    def landed(ref, n):
        pltpu.make_async_copy(ref, ref, recv.at[n]).wait()

    def sent(ref, n):
        pltpu.make_async_copy(ref, ref, send.at[n]).wait()

    pending = []

    def drain(count=None):
        for ref, n in pending[:count]:
            sent(ref, n)
        del pending[:count]

    def to_zc(src, dst, n):
        for j in far_first(zc_count):
            k = (zc + j) % zc_count
            push(src.at[:, k], dst.at[:, zc], n, at_zc(k))

        keep(src.at[:, zc], dst.at[:, zc], n)
        if zc_count > 1:
            pending.append((src.at[:, 0 : zc_count - 1], n))

    def to_y(src, dst, n):
        for j in far_first(ny):
            k = (y + j) % ny
            push(src.at[:, :, k], dst.at[:, :, y], n, at_y(k))

        keep(src.at[:, :, y], dst.at[:, :, y], n)
        if ny > 1:
            pending.append((src.at[:, :, 0 : ny - 1], n))

    load_o = pltpu.make_async_copy(owners_hbm, owners, local.at[5])
    load_s = pltpu.make_async_copy(slots_hbm, slots, local.at[6])
    load_b = pltpu.make_async_copy(bias_hbm, bias, local.at[7])
    load_g = [
        pltpu.make_async_copy(ref, table.at[a:b], local.at[8 + i])
        for i, (ref, a, b) in enumerate(
            ((means, 0, 3), (inv_scales, 3, 5), (correlation, 5, 6), (opacity, 6, 7))
        )
    ]
    load_o.start()
    load_s.start()
    load_f = pltpu.make_async_copy(features_hbm, feat, local.at[0])
    load_t = pltpu.make_async_copy(target_hbm, targ, local.at[1])
    load_w = pltpu.make_async_copy(weights_hbm, wts, local.at[2])

    barrier = pltpu.get_barrier_semaphore()

    for j in far_first(zc_count):
        pl.semaphore_signal(barrier, inc=1, device_id=at_zc((zc + j) % zc_count), device_id_type=MESH)

    for j in far_first(ny):
        pl.semaphore_signal(barrier, inc=1, device_id=at_y((y + j) % ny), device_id_type=MESH)

    for j in far_first(nx):
        pl.semaphore_signal(barrier, inc=1, device_id=at_x((v + j) % nx), device_id_type=MESH)

    pl.semaphore_signal(barrier, inc=1, device_id=up, device_id_type=MESH)
    pl.semaphore_signal(barrier, inc=1, device_id=down, device_id_type=MESH)

    def column(row):
        n = row.shape[1]
        same = iota((n, n), 0) == iota((n, n), 1)
        return jnp.sum(jnp.where(same, jnp.broadcast_to(row, (n, n)), 0.0), axis=1, keepdims=True)

    first = iota((entries, entries), 0)
    second = iota((entries, entries), 1)
    load_o.wait()
    owner = owners[...]
    home = ((owner % zc_count) * ny + owner // zc_count).astype(F32)
    home_col = column(home)
    alike = home_col == home
    rank_row = jnp.sum(jnp.where(alike & (first < second), 1.0, 0.0), axis=0, keepdims=True)
    at_home = jnp.where(iota((strips, entries), 0).astype(F32) == home, 1.0, 0.0).astype(BF16)
    load_s.wait()
    slot = slots[...].astype(F32)
    slot_high = jnp.floor(slot * (1.0 / 64.0))
    slot_low = slot - 64.0 * slot_high
    row_at = iota((width, entries), 0).astype(F32)
    sought = jnp.where(row_at == rank_row, slot_high, 0.0) + jnp.where(row_at - 8.0 == rank_row, slot_low, 0.0)
    sought = mm(at_home, sought.astype(BF16), 1, 1)
    fill(req, sought * 64.0 + pltpu.roll(sought, width - 8, 1))

    pl.semaphore_wait(barrier, zc_count + ny + nx - 3 + 2)

    to_zc(req, req_mid, 0)
    for load in load_g + [load_f, load_w, load_t, load_b]:
        load.start()
    push(target_hbm.at[0:16], halo_t.at[1], 1, up)
    push(target_hbm.at[pixels - 16 : pixels], halo_t.at[0], 1, down)
    pending.append((halo_t, 1))

    for load in load_g:
        load.wait()
    whole = jnp.concatenate([table[...], jnp.zeros((1, prims), F32)], axis=0)
    g_high, g_mid, g_low = (part.astype(F32) for part in split3(whole))
    g_parts[...] = jnp.concatenate(
        [g_high] * RANKS + [g_mid] * RANKS + [g_low] * RANKS + [jnp.zeros((32, prims), F32)], axis=0
    ).astype(BF16)
    load_f.wait()
    rows = min(prims, 512)

    @pl.loop(0, prims // rows)
    def _(i):
        here = pl.ds(pl.multiple_of(i * rows, rows), rows)
        high, low = split(feat[here, :])
        f_parts[here, 0:width] = high
        f_parts[here, width : 2 * width] = low

    landed(req_mid, 0)
    to_y(req_mid, req_got, 2)

    load_w.wait()
    for tap in range(9):
        high, low = split(wts[tap * width : (tap + 1) * width, :])
        w_parts[tap * width : (tap + 1) * width, 0:width] = high
        w_parts[tap * width : (tap + 1) * width, width : 2 * width] = low
        a, b = 2 - tap // 3, 2 - tap % 3
        w_turned[a, 0, :, b * width : (b + 1) * width] = high
        w_turned[a, 1, :, b * width : (b + 1) * width] = low
    load_t.wait()
    load_b.wait()
    rank_col = jnp.sum(jnp.where(alike & (second < first), 1.0, 0.0), axis=1, keepdims=True)
    place_row = rank_row * float(strips) + home
    place_col = rank_col * float(strips) + home_col
    to_place = jnp.where(iota((places, entries), 0).astype(F32) == place_row, 1.0, 0.0).astype(BF16)
    from_place = jnp.where(iota((entries, places), 1).astype(F32) == place_col, 1.0, 0.0).astype(BF16)
    before = jnp.where(first < second, 1.0, 0.0).astype(BF16)
    behind = jnp.where(first > second, 1.0, 0.0).astype(BF16)

    landed(req_got, 2)
    asked = rows_of(req_got, strips)
    square = jnp.concatenate([asked, jnp.zeros((width - strips, width), F32)], axis=0) if strips < width else asked
    asked_rows = jnp.transpose(square)[0:8, 0:strips]
    asked_all[v] = asked_rows

    for j in far_first(nx):
        push(asked_all.at[v], asked_all.at[v], 3, at_x((v + j) % nx))

    if nx > 1:
        pending.append((asked_all.at[0 : nx - 1], 3))

    block = min(prims, 256)
    ident = iota((1, block), 1).astype(F32).astype(BF16)
    packed = jnp.zeros((strips, width), F32)
    lanes = iota((strips, width), 1)
    for r in range(RANKS):
        for k in range(prims // block):
            near = (asked[:, r : r + 1] - float(k * block)).astype(BF16)
            onehot[r * strips : (r + 1) * strips, k * block : (k + 1) * block] = jnp.where(
                ident == near, jnp.ones((), BF16), jnp.zeros((), BF16)
            )
    for r in range(RANKS):
        found = mm(onehot[r * strips : (r + 1) * strips, :], g_parts[...], 1, 1)
        packed = packed + jnp.where((lanes % 32) // 8 == r, found, 0.0)

    def folded(x):
        x = x + pltpu.roll(x, width - 32, 1) + pltpu.roll(x, width - 64, 1)
        return jnp.where(lanes < 32, x, 0.0)

    fill(geo, folded(packed))
    to_zc(geo, geo_mid, 4)

    half = RANKS // 2
    pairs = (slice(0, half), slice(half, RANKS))
    for n, pair in enumerate(pairs):
        for r in range(pair.start, pair.stop):
            found = mm(onehot[r * strips : (r + 1) * strips, :], f_parts[...])
            fill(fea.at[r], found[:, 0:width] + found[:, width : 2 * width])
        (to_y if n else to_zc)(fea.at[pair], fea_mid.at[pair], 37 + n)
    landed(geo_mid, 4)
    to_y(geo_mid, geo_got, 7)
    for n, pair in enumerate(pairs):
        landed(fea_mid.at[pair], 37 + n)
        (to_zc if n else to_y)(fea_mid.at[pair], fea_got.at[pair], 41 + n)

    landed(geo_got, 7)

    def turned(x):
        x = jnp.concatenate([x, jnp.zeros((width - strips, width), F32)], axis=0) if strips < width else x
        return jnp.transpose(x)[0 : 8 * RANKS, 0:strips]

    def three(x):
        return jnp.concatenate([part.astype(F32) for part in split3(x)], axis=0).astype(BF16)

    spread = mm(three(turned(rows_of(geo_got, strips))), at_home)
    n8 = 8 * RANKS
    spread = spread[0:n8] + spread[n8 : 2 * n8] + spread[2 * n8 : 3 * n8]
    g = jnp.zeros((8, entries), F32)
    for r in range(RANKS):
        g = g + jnp.where(rank_row == float(r), spread[8 * r : 8 * r + 8, :], 0.0)

    def cam(axis, k):
        return cameras[0, axis, k]

    def center(axis):
        return 8.0 + 4.0 * (
            cam(axis, 0) * g[0:1] + cam(axis, 1) * g[1:2] + cam(axis, 2) * g[2:3] + cam(axis, 3)
        )

    pixel = iota((pixels, 1), 0)
    across = (pixel % 16).astype(F32) + 0.5
    downward = (pixel // 16).astype(F32) + 0.5
    du = across - center(0)
    dv = downward - center(1)
    a = g[3:4] * du
    b = g[4:5] * dv
    skew = g[5:6]
    grown = jnp.exp(-0.5 * (a * a + 2.0 * skew * a * b + b * b))
    solid = 1.0 / (1.0 + jnp.exp(-g[6:7]))
    raw = solid * grown
    alive = jnp.where(iota((1, entries), 1) < lengths[0, 0], 1.0, 0.0)
    cover = jnp.minimum(raw, 0.99) * alive
    fades = jnp.log(1.0 - cover)
    f_high, f_mid, f_low = split3(fades)
    through = jnp.exp(mm(f_high, before) + mm(f_mid, before) + mm(f_low, before))
    weight = cover * through
    weight_high, weight_low = split(weight)

    weight_t_high = jnp.transpose(weight_high.astype(F32)).astype(BF16)
    weight_t_low = jnp.transpose(weight_low.astype(F32)).astype(BF16)
    for n, pair in enumerate(pairs):
        landed(fea_got.at[pair], 41 + n)
    high, low = split(rows_of(fea_got, places))
    listed = mm(from_place, jnp.concatenate([high, low], axis=1)).astype(BF16)
    both = mm(weight_high, listed)
    tile = both[:, 0:width] + both[:, width:] + mm(weight_low, listed[:, 0:width])
    image[32 : 32 + pixels, :] = tile

    push(image.at[32:64], image.at[32 + pixels : 64 + pixels], 10, up)
    push(image.at[pixels : 32 + pixels], image.at[0:32], 10, down)
    pending.append((image.at[0:64], 10))

    def sideways(x):
        n = x.shape[0]
        col = iota((n, 1), 0) % 16
        left = jnp.where(col == 0, 0.0, pltpu.roll(x, 1, 0))
        right = jnp.where(col == 15, 0.0, pltpu.roll(x, n - 1, 0))
        return split(jnp.concatenate([left, x, right], axis=1))

    def taps(i):
        return w_parts[i * 3 * width : (i + 1) * 3 * width, :]

    def product(high, low, part):
        both = mm(high, part)
        return both[:, 0:width] + (both[:, width:] + mm(low, part[:, 0:width]))

    edge = jnp.zeros((32, width), F32)
    pic_high, pic_low = sideways(jnp.concatenate([edge, tile, edge], axis=0))
    decoded = jnp.zeros((extended, width), F32)
    for i in range(3):
        here = slice(i * 16, i * 16 + extended)
        decoded = decoded + product(pic_high[here, :], pic_low[here, :], taps(i))
    decoded = decoded + bias[...]
    pic_t_high = jnp.transpose(pic_high.astype(F32)).astype(BF16)
    pic_t_low = jnp.transpose(pic_low.astype(F32)).astype(BF16)
    drain()
    landed(halo_t, 1)
    aim = jnp.concatenate([halo_t[0], targ[...], halo_t[1]], axis=0)
    decoded = decoded - aim

    landed(image.at[0:64], 10)
    has_up = strip > 0
    has_down = strip < strips - 1
    beyond = jnp.concatenate([image[0:32, :], image[32 + pixels :, :]], axis=0)
    known = jnp.where(iota((64, 1), 0) < 32, has_up.astype(F32), has_down.astype(F32)) > 0.5
    out_high, out_low = sideways(jnp.where(known, beyond, 0.0))
    top = product(out_high[0:32, :], out_low[0:32, :], taps(0))
    mid = product(out_high[16:48, :], out_low[16:48, :], taps(1))
    low = product(out_high[32:64, :], out_low[32:64, :], taps(2))
    decoded = jnp.concatenate(
        [
            decoded[0:16] + (top[0:16] + mid[0:16]),
            decoded[16:32] + top[16:32],
            decoded[32 : extended - 32],
            decoded[extended - 32 : extended - 16] + low[0:16],
            decoded[extended - 16 :] + (low[16:32] + mid[16:32]),
        ],
        axis=0,
    )
    rows_at = iota((extended, 1), 0)
    inside = ((rows_at >= 16) | has_up) & ((rows_at < 16 + pixels) | has_down)
    residual = jnp.where(inside, decoded, 0.0)
    res_high, res_low = sideways(residual)
    own = residual[16 : 16 + pixels, :]
    shifted = []
    for i in range(3):
        shifted.append(
            jnp.concatenate(
                [jnp.zeros(((i + 1) * 16, width), F32), own, jnp.zeros((64 - (i + 1) * 16, width), F32)], axis=0
            )
        )
    own_high, own_low = split(jnp.concatenate(shifted, axis=1))
    w_grad = mm(pic_t_high, own_high) + (mm(pic_t_high, own_low) + mm(pic_t_low, own_high))
    next_high = jnp.concatenate([own_high[16:32], own_high[pixels + 32 : pixels + 48]], axis=0)
    next_low = jnp.concatenate([own_low[16:32], own_low[pixels + 32 : pixels + 48]], axis=0)
    near_high, near_low = out_high[16:48], out_low[16:48]
    w_grad = w_grad + (mm(near_high, next_high, 0, 0) + (mm(near_high, next_low, 0, 0) + mm(near_low, next_high, 0, 0)))
    for i in range(3):
        wl[i * 3 * width : (i + 1) * 3 * width, :] = w_grad[:, i * width : (i + 1) * width]
    b_grad = jnp.broadcast_to(jnp.sum(own, axis=0, keepdims=True), (8, width))
    rows_a, rows_b, pa, pb, ra, rb = decoder_rows(sizes)
    core_rows = rows_a + rows_b
    for k in range(nc):
        base = k * core_rows
        wx[k, 0:rows_a, :] = wl[base : base + rows_a, :]
        for i in range(ny):
            at = rows_a + i * (pb + 8)
            wx[k, at : at + pb, :] = wl[base + rows_a + i * pb : base + rows_a + (i + 1) * pb, :]
            wx[k, at + pb : at + pb + 8, :] = b_grad
    other = (v, y, z, 1 - c)
    push(wx.at[1 - c], wc, 15, other)
    pending.append((wc, 15))

    grad = jnp.zeros((pixels, width), F32)
    for i in range(3):
        here = slice(i * 16, i * 16 + pixels)
        grad = grad + (
            mm(res_high[here, :], w_turned[i, 0], 1, 1)
            + (mm(res_high[here, :], w_turned[i, 1], 1, 1) + mm(res_low[here, :], w_turned[i, 0], 1, 1))
        )
    grad_high, grad_low = split(grad)

    both = mm(weight_t_high, jnp.concatenate([grad_high, grad_low], axis=1))
    f_grad = both[:, 0:width] + (both[:, width:] + mm(weight_t_low, grad_high))
    high, low = split(f_grad)
    f_grad = jnp.concatenate([high, low], axis=1)
    for r in range(RANKS):
        both = mm(to_place[r * strips : (r + 1) * strips, :], f_grad)
        fill(back.at[r], both[:, 0:width] + both[:, width:])
    for n, pair in enumerate(pairs):
        (to_y if n else to_zc)(back.at[pair], back_mid.at[pair], 11 + n)

    d_weight = mm(jnp.concatenate([grad_high, grad_high], axis=1), listed, 1, 1) + mm(
        grad_low, listed[:, 0:width], 1, 1
    )
    f_high, f_mid, f_low = split3(d_weight * weight)
    later = mm(f_high, behind) + mm(f_mid, behind) + mm(f_low, behind)
    d_cover = d_weight * through - later / (1.0 - cover)
    d_raw = jnp.where(raw < 0.99, d_cover, 0.0) * alive
    d_grown = d_raw * raw
    u = (a + skew * b) * d_grown
    w = (b + skew * a) * d_grown

    def summed(x):
        return jnp.sum(x, axis=0, keepdims=True)

    d_col = 4.0 * g[3:4] * summed(u)
    d_row = 4.0 * g[4:5] * summed(w)
    parts = [cam(0, k) * d_col + cam(1, k) * d_row for k in range(3)]
    parts += [-summed(u * du), -summed(w * dv), -summed(d_grown * a * b), summed(d_grown) * (1.0 - solid)]
    parts.append(jnp.zeros((1, entries), F32))
    g_grad = jnp.concatenate(parts, axis=0)
    by_rank = jnp.concatenate([jnp.where(rank_row == float(r), g_grad, 0.0) for r in range(RANKS)], axis=0)
    by_rank = jnp.concatenate([part.astype(F32) for part in split3(by_rank)] + [jnp.zeros((32, entries), F32)], axis=0)
    fill(bgeo, folded(mm(at_home, by_rank.astype(BF16), 1, 1)))
    to_zc(bgeo, bgeo_mid, 16)

    landed(wc, 15)
    wa[...] = (wx[c, 0:rows_a, :] + wc[0:rows_a, :]).reshape(nz, pa, width)
    wb[...] = (wx[c, rows_a:, :] + wc[rows_a:, :]).reshape(ny, pb + 8, width)

    def along_z(src, dst, n):
        for j in far_first(nz):
            k = (z + j) % nz
            push(src(k), dst(z), n, (v, y, k, c))

    def along_y(src, dst, n):
        for j in far_first(ny):
            k = (y + j) % ny
            push(src(k), dst(y), n, at_y(k))

    def added(ref, n):
        sums = ref[0]
        for k in range(1, n):
            sums = sums + ref[k]
        return sums

    along_z(lambda k: wa.at[k], lambda k: wa_got.at[k], 17)
    keep(wa.at[z], wa_got.at[z], 17)
    along_y(lambda k: wb.at[k], lambda k: wb_got.at[k], 18)
    keep(wb.at[y], wb_got.at[y], 18)
    if nz > 1:
        pending.append((wa.at[0 : nz - 1], 17))
    if ny > 1:
        pending.append((wb.at[0 : ny - 1], 18))

    for n, pair in enumerate(pairs):
        landed(back_mid.at[pair], 11 + n)
        (to_zc if n else to_y)(back_mid.at[pair], back_got.at[pair], 19 + n)
    landed(bgeo_mid, 16)
    to_y(bgeo_mid, bgeo_got, 23)

    landed(wa_got, 17)
    sums = added(wa_got, nz)
    for k in range(ny):
        fill(wa2.at[k], sums[k * ra : (k + 1) * ra, :])
    along_y(lambda k: wa2.at[k], lambda k: wa2_got.at[k], 24)
    keep(wa2.at[y], wa2_got.at[y], 24)
    landed(wb_got, 18)
    sums = added(wb_got, ny)
    for k in range(nz):
        fill(wb2.at[k, 0:rb], sums[k * rb : (k + 1) * rb, :])
        fill(wb2.at[k, rb : rb + 1], sums[pb : pb + 1, :])
    along_z(lambda k: wb2.at[k], lambda k: wb2_got.at[k], 25)
    keep(wb2.at[z], wb2_got.at[z], 25)
    if ny > 1:
        pending.append((wa2.at[0 : ny - 1], 24))
    if nz > 1:
        pending.append((wb2.at[0 : nz - 1], 25))

    def to_x(src, dst, n):
        for j in far_first(nx):
            push(src, dst, n, at_x((v + j) % nx))

        keep(src, dst, n)
        for _ in range(nx - 1):
            pending.append((src, n))

    def plane(r):
        return all_f.at[v, r]

    older = len(pending)
    landed(back_got.at[0:half], 19)
    to_x(back_got.at[0], plane(0), 26)
    landed(bgeo_got, 23)
    own_g[...] = turned(rows_of(bgeo_got, strips))
    to_x(own_g, all_g.at[v], 30)

    landed(wa2_got, 24)
    landed(wb2_got, 25)
    wq[0:ra] = added(wa2_got, ny)
    wq[ra:] = added(wb2_got, nz)
    to_x(wq, wq_got.at[v], 31)
    for r in range(1, RANKS):
        if r == half:
            landed(back_got.at[half:RANKS], 20)
        to_x(back_got.at[r], plane(r), 26 + r)

    if nx > 1:
        landed(asked_all.at[0 : nx - 1], 3)
    slot_at = iota((block, 1), 0).astype(F32).astype(BF16)

    def geometry_of(r):
        return three(jnp.concatenate([shared_g[k][8 * r : 8 * r + 8, :] for k in range(nx)], axis=1))

    def scatter(r):
        asks = jnp.concatenate([asked_all[k][r : r + 1, :] for k in range(nx)], axis=1)
        came_g = geometry_of(r)
        high, low = split(jnp.concatenate([rows_of(all_f.at[k, r], strips) for k in range(nx)], axis=0))
        came = jnp.concatenate([high, low], axis=1)

        @pl.loop(0, prims // rows)
        def _(i):
            here = pl.ds(pl.multiple_of(i * rows, rows), rows)
            base = (i * rows).astype(F32)
            hits = jnp.concatenate(
                [
                    jnp.where(
                        slot_at == (asks - (base + float(k * block))).astype(BF16),
                        jnp.ones((), BF16),
                        jnp.zeros((), BF16),
                    )
                    for k in range(rows // block)
                ],
                axis=0,
            )
            both = mm(hits, came)
            both = both[:, 0:width] + both[:, width:]
            found = mm(came_g, hits, 1, 1)
            found = found[0:8] + found[8:16] + found[16:24]
            if r:
                total[here, :] += both
                total_g[i] += found
            else:
                total[here, :] = both
                total_g[i] = found

    drain(older)
    landed(wq_got, 31)
    sums = added(wq_got, nx)
    b_total[...] = sums[ra + rb]
    save_b = pltpu.make_async_copy(b_total, bias_out, local.at[4])
    save_b.start()
    wa3[y] = sums[0:ra]
    wb3[z] = sums[ra : ra + rb]
    along_y(lambda k: wa3.at[y], lambda k: wa3.at[k], 32)
    along_z(lambda k: wb3.at[z], lambda k: wb3.at[k], 33)
    if ny > 1:
        pending.append((wa3.at[0 : ny - 1], 32))
    if nz > 1:
        pending.append((wb3.at[0 : nz - 1], 33))

    landed(all_g, 30)
    shared_g = [all_g[k] for k in range(nx)]
    landed(all_f.at[:, 0], 26)
    scatter(0)

    landed(all_f.at[:, 1], 27)
    scatter(1)

    if ny > 1:
        landed(wa3.at[0 : ny - 1], 32)
    if nz > 1:
        landed(wb3.at[0 : nz - 1], 33)

    def part_a(k):
        return weight_out.at[c, pl.ds(pl.multiple_of(k * pa, 8), pa)]

    def part_b(k):
        return weight_out.at[c, pl.ds(pl.multiple_of(rows_a + k * pb, 8), pb)]

    mine_a[...] = rows_of(wa3, pa)
    mine_b[...] = rows_of(wb3, pb)
    along_z(lambda k: mine_a, part_a, 34)
    along_y(lambda k: mine_b, part_b, 35)
    keep(mine_a, part_a(z), 34)
    keep(mine_b, part_b(y), 35)
    drain()
    for _ in range(nz - 1):
        pending.append((mine_a, 34))
    for _ in range(ny - 1):
        pending.append((mine_b, 35))

    landed(all_f.at[:, 2], 28)
    scatter(2)
    landed(all_f.at[:, 3], 29)
    scatter(3)
    save_f = pltpu.make_async_copy(total, feature_out, local.at[3])
    save_f.start()
    for i in range(prims // rows):
        g_total[:, i * rows : (i + 1) * rows] = total_g[i][0:7]
    save_g = pltpu.make_async_copy(g_total, geometry_out, local.at[2])
    save_g.start()

    drain()
    landed(weight_out.at[c, 0:rows_a], 34)
    landed(weight_out.at[c, rows_a:], 35)
    push(weight_out.at[c], weight_out.at[c], 36, other)
    pending.append((weight_out.at[0], 36))
    landed(weight_out.at[0], 36)
    drain()
    save_f.wait()
    save_g.wait()
    save_b.wait()


def decoder_rows(sizes):
    nx, ny, nz, nc, entries, prims, height = sizes
    rows = 9 * 128 // nc
    rows_a = rows * 5 // 9
    rows_b = rows - rows_a
    return rows_a, rows_b, rows_a // nz, rows_b // ny, rows_a // nz // ny, rows_b // nz // ny


def passing(count, *refs):
    moves = [pltpu.make_async_copy(refs[i], refs[count + i], refs[-1].at[i]) for i in range(count)]
    for move in moves:
        move.start()
    for move in moves:
        move.wait()


def hand_over(*arrays):
    any_ = pl.BlockSpec(memory_space=pl.ANY)
    return pl.pallas_call(
        functools.partial(passing, len(arrays)),
        name="hand_over",
        out_shape=tuple(jax.ShapeDtypeStruct(a.shape, a.dtype) for a in arrays),
        in_specs=[any_] * len(arrays),
        out_specs=(any_,) * len(arrays),
        scratch_shapes=[pltpu.SemaphoreType.DMA((len(arrays),))],
        compiler_params=pltpu.CompilerParams(vmem_limit_bytes=1024 * 1024),
    )(*arrays)


def per_device(sizes, *arrays):
    means, inv_scales, correlation, opacity, features, cameras, owners, slots, lengths, target, weights, bias = arrays
    nx, ny, nz, nc, entries, prims, height = sizes
    zc = nz * nc
    strips = ny * zc
    width = 128
    pixels = height * 16
    rows = min(prims, 512)
    rows_a, rows_b, pa, pb, ra, rb = decoder_rows(sizes)
    smem = pl.BlockSpec(memory_space=pltpu.SMEM)
    any_ = pl.BlockSpec(memory_space=pl.ANY)
    hbm = pl.BlockSpec(memory_space=pltpu.HBM)

    def f32(*shape):
        return pltpu.VMEM(shape, F32)

    def planes(n):
        return f32(n, zc, ny, 1, width)

    geometry, feature, weight, b_grad = pl.pallas_call(
        functools.partial(kernel, sizes),
        name="splat_step",
        out_shape=(
            jax.ShapeDtypeStruct((7, prims), F32),
            jax.ShapeDtypeStruct((prims, width), F32),
            jax.ShapeDtypeStruct((nc, rows_a + rows_b, width), F32),
            jax.ShapeDtypeStruct((1, width), F32),
        ),
        in_specs=[hbm] * 4 + [smem, hbm, hbm, smem, hbm] + [hbm] * 3,
        out_specs=(any_,) * 4,
        scratch_shapes=[
            pltpu.VMEM((1, entries), jnp.int32), pltpu.VMEM((1, entries), jnp.int32), f32(1, width),
            f32(prims, width), f32(pixels, width), f32(9 * width, width), f32(7, prims),
            pltpu.VMEM((width, prims), BF16), pltpu.VMEM((prims, 2 * width), BF16),
            pltpu.VMEM((9 * width, 2 * width), BF16), pltpu.VMEM((3, 2, width, 3 * width), BF16),
            pltpu.VMEM((RANKS * strips, prims), BF16), f32(2, 16, width),
            planes(1), planes(1), planes(1), f32(nx, 8, strips),
            planes(1), planes(1), planes(1), planes(RANKS), planes(RANKS), planes(RANKS),
            f32(pixels + 64, width), planes(RANKS), planes(RANKS), planes(RANKS), planes(1), planes(1), planes(1),
            f32(nx, RANKS, zc, ny, 1, width), f32(nx, 8 * RANKS, strips), f32(8 * RANKS, strips),
            f32(prims, width), f32(prims // rows, 8, rows), f32(9 * width, width),
            f32(nc, rows_a + rows_b + 8 * ny, width), f32(rows_a + rows_b + 8 * ny, width),
            f32(nz, pa, width), f32(nz, pa, width), f32(ny, pb + 8, width), f32(ny, pb + 8, width),
            f32(ny, ra, 1, width), f32(ny, ra, 1, width), f32(nz, rb + 1, 1, width), f32(nz, rb + 1, 1, width),
            f32(ra + rb + 1, 1, width), f32(nx, ra + rb + 1, 1, width),
            f32(ny, ra, 1, width), f32(nz, rb, 1, width), f32(pa, width), f32(pb, width), f32(7, prims), f32(1, width),
            pltpu.SemaphoreType.DMA((45,)), pltpu.SemaphoreType.DMA((45,)), pltpu.SemaphoreType.DMA((12,)),
        ],
        compiler_params=pltpu.CompilerParams(
            collective_id=0, has_side_effects=True, vmem_limit_bytes=VMEM_LIMIT
        ),
    )(
        *[a if n == 7 else pltpu.with_memory_space_constraint(a, pltpu.HBM) for n, a in enumerate((
        means, inv_scales, correlation.reshape(1, prims), opacity.reshape(1, prims), cameras,
        owners.reshape(1, entries), slots.reshape(1, entries), lengths.reshape(1, 1), bias.reshape(1, width),
        features, target.reshape(pixels, width), weights.reshape(9 * width, width),
        ))],
    )
    geometry, feature, weight, b_grad = hand_over(geometry, feature, weight.reshape(9 * width, width), b_grad)
    return geometry, feature, weight.reshape(3, 3, width, width), b_grad.reshape(width)


def built(mesh, ny, nz, nc, entries, prims, height):
    nx = mesh.shape["view"]
    finer = Mesh(mesh.devices.reshape(nx, ny, nz, nc), ("view",) + STRIP)
    return jax.shard_map(
        functools.partial(per_device, (nx, ny, nz, nc, entries, prims, height)),
        mesh=finer,
        in_specs=(
            P(None, STRIP),
            P(None, STRIP),
            P(STRIP),
            P(STRIP),
            P(STRIP, None),
            P("view", None, None),
            P("view", STRIP, None, None),
            P("view", STRIP, None),
            P("view", STRIP),
            P("view", STRIP, None, None),
            P(),
            P(),
        ),
        out_specs=(P(None, STRIP), P(STRIP, None), P(), P()),
        check_vma=False,
    )


def solution(mesh):
    return built(mesh, 8, 8, 2, 256, 2048, 16)
```

```python
import functools

import jax
import jax.numpy as jnp
from jax import lax
from jax.experimental import pallas as pl
from jax.experimental.pallas import tpu as pltpu
from jax.sharding import Mesh
from jax.sharding import PartitionSpec as P

STRIP = ("strip_0", "strip_1", "strip_2")
MESH = pl.DeviceIdType.MESH
F32 = jnp.float32
BF16 = jnp.bfloat16
VMEM_LIMIT = 24 * 1024 * 1024
RANKS = 4


def iota(shape, dim):
    return lax.broadcasted_iota(jnp.int32, shape, dim)


def mm(a, b, ca=1, cb=0):
    return lax.dot_general(a, b, (((ca,), (cb,)), ((), ())), preferred_element_type=F32)


def split(x):
    high = x.astype(BF16)
    return high, (x - high.astype(F32)).astype(BF16)


def split3(x):
    high = x.astype(BF16)
    rest = x - high.astype(F32)
    mid = rest.astype(BF16)
    return high, mid, (rest - mid.astype(F32)).astype(BF16)


def far_first(n):
    return sorted(range(1, n), key=lambda j: -min(j, n - j))


def rows_of(ref, n):
    return ref.reshape(n, ref.shape[-1])[...]


def fill(ref, value):
    ref.reshape(*value.shape)[...] = value


def kernel(
    sizes,
    means, inv_scales, correlation, opacity, cameras_hbm, owners_hbm, slots_hbm, lengths, bias_hbm,
    features_hbm, target_hbm, weights_hbm,
    geometry_out, feature_out, weight_out, bias_out,
    owners, slots, bias, cameras, feat, targ, wts, table, g_parts, f_parts, w_parts, w_turned, onehot, halo_t,
    req, req_mid, req_got, asked_all,
    geo, geo_mid, geo_got, fea, fea_mid, fea_got,
    image, back, back_mid, back_got, bgeo, bgeo_mid, bgeo_got, all_f, all_g, own_g,
    total, total_g, wl, wx, wc, wa, wa_got, wb, wb_got, wa2, wa2_got, wb2, wb2_got, wq, wq_got, wa3, wb3, mine_a, mine_b, g_total, b_total,
    send, recv, local,
):
    nx, ny, nz, nc, entries, prims, height = sizes
    zc_count = nz * nc
    strips = ny * zc_count
    places = RANKS * strips
    width = 128
    pixels = height * 16
    extended = pixels + 32
    v = lax.axis_index("view")
    y = lax.axis_index("strip_0")
    z = lax.axis_index("strip_1")
    c = lax.axis_index("strip_2")
    zc = z * nc + c
    strip = y * zc_count + zc

    def at_zc(k):
        return (v, y, k // nc, k % nc)

    def at_y(k):
        return (v, k, z, c)

    def at_x(k):
        return (k, y, z, c)

    def at_strip(k):
        return (v, k // zc_count, (k % zc_count) // nc, k % nc)

    up = at_strip((strip + strips - 1) % strips)
    down = at_strip((strip + 1) % strips)

    def push(src, dst, n, device):
        pltpu.make_async_remote_copy(
            src_ref=src, dst_ref=dst, send_sem=send.at[n], recv_sem=recv.at[n],
            device_id=device, device_id_type=MESH,
        ).start()

    def keep(src, dst, n):
        pltpu.make_async_copy(src, dst, recv.at[n]).start()

    def landed(ref, n):
        pltpu.make_async_copy(ref, ref, recv.at[n]).wait()

    def sent(ref, n):
        pltpu.make_async_copy(ref, ref, send.at[n]).wait()

    pending = []

    def drain(count=None):
        for ref, n in pending[:count]:
            sent(ref, n)
        del pending[:count]

    def to_zc(src, dst, n):
        for j in far_first(zc_count):
            k = (zc + j) % zc_count
            push(src.at[:, k], dst.at[:, zc], n, at_zc(k))

        keep(src.at[:, zc], dst.at[:, zc], n)
        if zc_count > 1:
            pending.append((src.at[:, 0 : zc_count - 1], n))

    def to_y(src, dst, n):
        for j in far_first(ny):
            k = (y + j) % ny
            push(src.at[:, :, k], dst.at[:, :, y], n, at_y(k))

        keep(src.at[:, :, y], dst.at[:, :, y], n)
        if ny > 1:
            pending.append((src.at[:, :, 0 : ny - 1], n))

    load_o = pltpu.make_async_copy(owners_hbm, owners, local.at[5])
    load_s = pltpu.make_async_copy(slots_hbm, slots, local.at[6])
    load_b = pltpu.make_async_copy(bias_hbm, bias, local.at[7])
    load_c = pltpu.make_async_copy(cameras_hbm, cameras, local.at[12])
    load_g = [
        pltpu.make_async_copy(ref, table.at[a:b], local.at[8 + i])
        for i, (ref, a, b) in enumerate(
            ((means, 0, 3), (inv_scales, 3, 5), (correlation, 5, 6), (opacity, 6, 7))
        )
    ]
    load_o.start()
    load_s.start()
    load_f = pltpu.make_async_copy(features_hbm, feat, local.at[0])
    load_t = pltpu.make_async_copy(target_hbm, targ, local.at[1])
    load_w = pltpu.make_async_copy(weights_hbm, wts, local.at[2])

    barrier = pltpu.get_barrier_semaphore()

    for j in far_first(zc_count):
        pl.semaphore_signal(barrier, inc=1, device_id=at_zc((zc + j) % zc_count), device_id_type=MESH)

    for j in far_first(ny):
        pl.semaphore_signal(barrier, inc=1, device_id=at_y((y + j) % ny), device_id_type=MESH)

    for j in far_first(nx):
        pl.semaphore_signal(barrier, inc=1, device_id=at_x((v + j) % nx), device_id_type=MESH)

    pl.semaphore_signal(barrier, inc=1, device_id=up, device_id_type=MESH)
    pl.semaphore_signal(barrier, inc=1, device_id=down, device_id_type=MESH)

    def column(row):
        n = row.shape[1]
        same = iota((n, n), 0) == iota((n, n), 1)
        return jnp.sum(jnp.where(same, jnp.broadcast_to(row, (n, n)), 0.0), axis=1, keepdims=True)

    first = iota((entries, entries), 0)
    second = iota((entries, entries), 1)
    load_o.wait()
    owner = owners[...]
    home = ((owner % zc_count) * ny + owner // zc_count).astype(F32)
    home_col = column(home)
    alike = home_col == home
    rank_row = jnp.sum(jnp.where(alike & (first < second), 1.0, 0.0), axis=0, keepdims=True)
    at_home = jnp.where(iota((strips, entries), 0).astype(F32) == home, 1.0, 0.0).astype(BF16)
    load_s.wait()
    slot = slots[...].astype(F32)
    slot_high = jnp.floor(slot * (1.0 / 64.0))
    slot_low = slot - 64.0 * slot_high
    row_at = iota((width, entries), 0).astype(F32)
    sought = jnp.where(row_at == rank_row, slot_high, 0.0) + jnp.where(row_at - 8.0 == rank_row, slot_low, 0.0)
    sought = mm(at_home, sought.astype(BF16), 1, 1)
    fill(req, sought * 64.0 + pltpu.roll(sought, width - 8, 1))

    pl.semaphore_wait(barrier, zc_count + ny + nx - 3 + 2)

    to_zc(req, req_mid, 0)
    for load in load_g + [load_f, load_w, load_t, load_b, load_c]:
        load.start()
    push(target_hbm.at[0:16], halo_t.at[1], 1, up)
    push(target_hbm.at[pixels - 16 : pixels], halo_t.at[0], 1, down)
    pending.append((halo_t, 1))

    for load in load_g:
        load.wait()
    whole = jnp.concatenate([table[...], jnp.zeros((1, prims), F32)], axis=0)
    g_high, g_mid, g_low = (part.astype(F32) for part in split3(whole))
    g_parts[...] = jnp.concatenate(
        [g_high] * RANKS + [g_mid] * RANKS + [g_low] * RANKS + [jnp.zeros((32, prims), F32)], axis=0
    ).astype(BF16)
    load_f.wait()
    rows = min(prims, 512)

    @pl.loop(0, prims // rows)
    def _(i):
        here = pl.ds(pl.multiple_of(i * rows, rows), rows)
        high, low = split(feat[here, :])
        f_parts[here, 0:width] = high
        f_parts[here, width : 2 * width] = low

    landed(req_mid, 0)
    to_y(req_mid, req_got, 2)

    load_w.wait()
    for tap in range(9):
        high, low = split(wts[tap * width : (tap + 1) * width, :])
        w_parts[tap * width : (tap + 1) * width, 0:width] = high
        w_parts[tap * width : (tap + 1) * width, width : 2 * width] = low
        a, b = 2 - tap // 3, 2 - tap % 3
        w_turned[a, 0, :, b * width : (b + 1) * width] = high
        w_turned[a, 1, :, b * width : (b + 1) * width] = low
    load_t.wait()
    load_b.wait()
    load_c.wait()
    rank_col = jnp.sum(jnp.where(alike & (second < first), 1.0, 0.0), axis=1, keepdims=True)
    place_row = rank_row * float(strips) + home
    place_col = rank_col * float(strips) + home_col
    to_place = jnp.where(iota((places, entries), 0).astype(F32) == place_row, 1.0, 0.0).astype(BF16)
    from_place = jnp.where(iota((entries, places), 1).astype(F32) == place_col, 1.0, 0.0).astype(BF16)
    before = jnp.where(first < second, 1.0, 0.0).astype(BF16)
    behind = jnp.where(first > second, 1.0, 0.0).astype(BF16)

    landed(req_got, 2)
    asked = rows_of(req_got, strips)
    block = min(prims, 256)
    ident = iota((1, block), 1).astype(F32).astype(BF16)
    packed = jnp.zeros((strips, width), F32)
    lanes = iota((strips, width), 1)
    for r in range(RANKS):
        for k in range(prims // block):
            near = (asked[:, r : r + 1] - float(k * block)).astype(BF16)
            onehot[r * strips : (r + 1) * strips, k * block : (k + 1) * block] = jnp.where(
                ident == near, jnp.ones((), BF16), jnp.zeros((), BF16)
            )
    for r in range(RANKS):
        found = mm(onehot[r * strips : (r + 1) * strips, :], g_parts[...], 1, 1)
        packed = packed + jnp.where((lanes % 32) // 8 == r, found, 0.0)

    def folded(x):
        x = x + pltpu.roll(x, width - 32, 1) + pltpu.roll(x, width - 64, 1)
        return jnp.where(lanes < 32, x, 0.0)

    fill(geo, folded(packed))
    to_zc(geo, geo_mid, 4)

    half = RANKS // 2
    pairs = (slice(0, half), slice(half, RANKS))
    for n, pair in enumerate(pairs):
        for r in range(pair.start, pair.stop):
            found = mm(onehot[r * strips : (r + 1) * strips, :], f_parts[...])
            fill(fea.at[r], found[:, 0:width] + found[:, width : 2 * width])
        (to_y if n else to_zc)(fea.at[pair], fea_mid.at[pair], 37 + n)
    square = jnp.concatenate([asked, jnp.zeros((width - strips, width), F32)], axis=0) if strips < width else asked
    asked_rows = jnp.transpose(square)[0:8, 0:strips]
    asked_all[v] = asked_rows

    for j in far_first(nx):
        push(asked_all.at[v], asked_all.at[v], 3, at_x((v + j) % nx))

    if nx > 1:
        pending.append((asked_all.at[0 : nx - 1], 3))

    landed(geo_mid, 4)
    to_y(geo_mid, geo_got, 7)
    for n, pair in enumerate(pairs):
        landed(fea_mid.at[pair], 37 + n)
        (to_zc if n else to_y)(fea_mid.at[pair], fea_got.at[pair], 41 + n)

    landed(geo_got, 7)

    def turned(x):
        x = jnp.concatenate([x, jnp.zeros((width - strips, width), F32)], axis=0) if strips < width else x
        return jnp.transpose(x)[0 : 8 * RANKS, 0:strips]

    def three(x):
        return jnp.concatenate([part.astype(F32) for part in split3(x)], axis=0).astype(BF16)

    spread = mm(three(turned(rows_of(geo_got, strips))), at_home)
    n8 = 8 * RANKS
    spread = spread[0:n8] + spread[n8 : 2 * n8] + spread[2 * n8 : 3 * n8]
    g = jnp.zeros((8, entries), F32)
    for r in range(RANKS):
        g = g + jnp.where(rank_row == float(r), spread[8 * r : 8 * r + 8, :], 0.0)

    def cam(axis, k):
        return cameras[0, axis : axis + 1, k : k + 1]

    def center(axis):
        return 8.0 + 4.0 * (
            cam(axis, 0) * g[0:1] + cam(axis, 1) * g[1:2] + cam(axis, 2) * g[2:3] + cam(axis, 3)
        )

    pixel = iota((pixels, 1), 0)
    across = (pixel % 16).astype(F32) + 0.5
    downward = (pixel // 16).astype(F32) + 0.5
    du = across - center(0)
    dv = downward - center(1)
    a = g[3:4] * du
    b = g[4:5] * dv
    skew = g[5:6]
    grown = jnp.exp(-0.5 * (a * a + 2.0 * skew * a * b + b * b))
    solid = 1.0 / (1.0 + jnp.exp(-g[6:7]))
    raw = solid * grown
    alive = jnp.where(iota((1, entries), 1) < lengths[0, 0], 1.0, 0.0)
    cover = jnp.minimum(raw, 0.99) * alive
    fades = jnp.log(1.0 - cover)
    f_high, f_mid, f_low = split3(fades)
    through = jnp.exp(mm(f_high, before) + mm(f_mid, before) + mm(f_low, before))
    weight = cover * through
    weight_high, weight_low = split(weight)

    weight_t_high = jnp.transpose(weight_high.astype(F32)).astype(BF16)
    weight_t_low = jnp.transpose(weight_low.astype(F32)).astype(BF16)
    for n, pair in enumerate(pairs):
        landed(fea_got.at[pair], 41 + n)
    high, low = split(rows_of(fea_got, places))
    listed = mm(from_place, jnp.concatenate([high, low], axis=1)).astype(BF16)
    both = mm(weight_high, listed)
    tile = both[:, 0:width] + both[:, width:] + mm(weight_low, listed[:, 0:width])
    image[32 : 32 + pixels, :] = tile

    push(image.at[32:64], image.at[32 + pixels : 64 + pixels], 10, up)
    push(image.at[pixels : 32 + pixels], image.at[0:32], 10, down)
    pending.append((image.at[0:64], 10))

    def sideways(x):
        n = x.shape[0]
        col = iota((n, 1), 0) % 16
        left = jnp.where(col == 0, 0.0, pltpu.roll(x, 1, 0))
        right = jnp.where(col == 15, 0.0, pltpu.roll(x, n - 1, 0))
        return split(jnp.concatenate([left, x, right], axis=1))

    def taps(i):
        return w_parts[i * 3 * width : (i + 1) * 3 * width, :]

    def product(high, low, part):
        both = mm(high, part)
        return both[:, 0:width] + (both[:, width:] + mm(low, part[:, 0:width]))

    edge = jnp.zeros((32, width), F32)
    pic_high, pic_low = sideways(jnp.concatenate([edge, tile, edge], axis=0))
    decoded = jnp.zeros((extended, width), F32)
    for i in range(3):
        here = slice(i * 16, i * 16 + extended)
        decoded = decoded + product(pic_high[here, :], pic_low[here, :], taps(i))
    decoded = decoded + bias[...]
    pic_t_high = jnp.transpose(pic_high.astype(F32)).astype(BF16)
    pic_t_low = jnp.transpose(pic_low.astype(F32)).astype(BF16)
    drain()
    landed(halo_t, 1)
    aim = jnp.concatenate([halo_t[0], targ[...], halo_t[1]], axis=0)
    decoded = decoded - aim

    landed(image.at[0:64], 10)
    has_up = strip > 0
    has_down = strip < strips - 1
    beyond = jnp.concatenate([image[0:32, :], image[32 + pixels :, :]], axis=0)
    known = jnp.where(iota((64, 1), 0) < 32, has_up.astype(F32), has_down.astype(F32)) > 0.5
    out_high, out_low = sideways(jnp.where(known, beyond, 0.0))
    top = product(out_high[0:32, :], out_low[0:32, :], taps(0))
    mid = product(out_high[16:48, :], out_low[16:48, :], taps(1))
    low = product(out_high[32:64, :], out_low[32:64, :], taps(2))
    decoded = jnp.concatenate(
        [
            decoded[0:16] + (top[0:16] + mid[0:16]),
            decoded[16:32] + top[16:32],
            decoded[32 : extended - 32],
            decoded[extended - 32 : extended - 16] + low[0:16],
            decoded[extended - 16 :] + (low[16:32] + mid[16:32]),
        ],
        axis=0,
    )
    rows_at = iota((extended, 1), 0)
    inside = ((rows_at >= 16) | has_up) & ((rows_at < 16 + pixels) | has_down)
    residual = jnp.where(inside, decoded, 0.0)
    res_high, res_low = sideways(residual)
    own = residual[16 : 16 + pixels, :]
    shifted = []
    for i in range(3):
        shifted.append(
            jnp.concatenate(
                [jnp.zeros(((i + 1) * 16, width), F32), own, jnp.zeros((64 - (i + 1) * 16, width), F32)], axis=0
            )
        )
    own_high, own_low = split(jnp.concatenate(shifted, axis=1))
    w_grad = mm(pic_t_high, own_high) + (mm(pic_t_high, own_low) + mm(pic_t_low, own_high))
    next_high = jnp.concatenate([own_high[16:32], own_high[pixels + 32 : pixels + 48]], axis=0)
    next_low = jnp.concatenate([own_low[16:32], own_low[pixels + 32 : pixels + 48]], axis=0)
    near_high, near_low = out_high[16:48], out_low[16:48]
    w_grad = w_grad + (mm(near_high, next_high, 0, 0) + (mm(near_high, next_low, 0, 0) + mm(near_low, next_high, 0, 0)))
    for i in range(3):
        wl[i * 3 * width : (i + 1) * 3 * width, :] = w_grad[:, i * width : (i + 1) * width]
    b_grad = jnp.broadcast_to(jnp.sum(own, axis=0, keepdims=True), (8, width))
    rows_a, rows_b, pa, pb, ra, rb = decoder_rows(sizes)
    core_rows = rows_a + rows_b
    for k in range(nc):
        base = k * core_rows
        wx[k, 0:rows_a, :] = wl[base : base + rows_a, :]
        for i in range(ny):
            at = rows_a + i * (pb + 8)
            wx[k, at : at + pb, :] = wl[base + rows_a + i * pb : base + rows_a + (i + 1) * pb, :]
            wx[k, at + pb : at + pb + 8, :] = b_grad
    other = (v, y, z, 1 - c)
    push(wx.at[1 - c, 0:rows_a], wc.at[0:rows_a], 15, other)
    push(wx.at[1 - c, rows_a:], wc.at[rows_a:], 45, other)
    pending.append((wc.at[0:rows_a], 15))
    pending.append((wc.at[rows_a:], 45))

    grad = jnp.zeros((pixels, width), F32)
    for i in range(3):
        here = slice(i * 16, i * 16 + pixels)
        grad = grad + (
            mm(res_high[here, :], w_turned[i, 0], 1, 1)
            + (mm(res_high[here, :], w_turned[i, 1], 1, 1) + mm(res_low[here, :], w_turned[i, 0], 1, 1))
        )
    grad_high, grad_low = split(grad)

    both = mm(weight_t_high, jnp.concatenate([grad_high, grad_low], axis=1))
    f_grad = both[:, 0:width] + (both[:, width:] + mm(weight_t_low, grad_high))
    high, low = split(f_grad)
    f_grad = jnp.concatenate([high, low], axis=1)
    for r in range(RANKS):
        both = mm(to_place[r * strips : (r + 1) * strips, :], f_grad)
        fill(back.at[r], both[:, 0:width] + both[:, width:])
    for n, pair in enumerate(pairs):
        (to_y if n else to_zc)(back.at[pair], back_mid.at[pair], 11 + n)


    def along_z(src, dst, n):
        for j in far_first(nz):
            k = (z + j) % nz
            push(src(k), dst(z), n, (v, y, k, c))

    def along_y(src, dst, n):
        for j in far_first(ny):
            k = (y + j) % ny
            push(src(k), dst(y), n, at_y(k))

    def added(ref, n):
        sums = ref[0]
        for k in range(1, n):
            sums = sums + ref[k]
        return sums

    landed(wc.at[0:rows_a], 15)
    wa[...] = (wx[c, 0:rows_a, :] + wc[0:rows_a, :]).reshape(nz, pa, width)
    along_z(lambda k: wa.at[k], lambda k: wa_got.at[k], 17)
    keep(wa.at[z], wa_got.at[z], 17)

    d_weight = mm(jnp.concatenate([grad_high, grad_high], axis=1), listed, 1, 1) + mm(
        grad_low, listed[:, 0:width], 1, 1
    )
    f_high, f_mid, f_low = split3(d_weight * weight)
    later = mm(f_high, behind) + mm(f_mid, behind) + mm(f_low, behind)
    d_cover = d_weight * through - later / (1.0 - cover)
    d_raw = jnp.where(raw < 0.99, d_cover, 0.0) * alive
    d_grown = d_raw * raw
    u = (a + skew * b) * d_grown
    w = (b + skew * a) * d_grown

    def summed(x):
        return jnp.sum(x, axis=0, keepdims=True)

    d_col = 4.0 * g[3:4] * summed(u)
    d_row = 4.0 * g[4:5] * summed(w)
    parts = [cam(0, k) * d_col + cam(1, k) * d_row for k in range(3)]
    parts += [-summed(u * du), -summed(w * dv), -summed(d_grown * a * b), summed(d_grown) * (1.0 - solid)]
    parts.append(jnp.zeros((1, entries), F32))
    g_grad = jnp.concatenate(parts, axis=0)
    by_rank = jnp.concatenate([jnp.where(rank_row == float(r), g_grad, 0.0) for r in range(RANKS)], axis=0)
    by_rank = jnp.concatenate([part.astype(F32) for part in split3(by_rank)] + [jnp.zeros((32, entries), F32)], axis=0)
    fill(bgeo, folded(mm(at_home, by_rank.astype(BF16), 1, 1)))
    landed(wc.at[rows_a:], 45)
    wb[...] = (wx[c, rows_a:, :] + wc[rows_a:, :]).reshape(ny, pb + 8, width)
    along_y(lambda k: wb.at[k], lambda k: wb_got.at[k], 18)
    keep(wb.at[y], wb_got.at[y], 18)
    to_zc(bgeo, bgeo_mid, 16)
    if nz > 1:
        pending.append((wa.at[0 : nz - 1], 17))
    if ny > 1:
        pending.append((wb.at[0 : ny - 1], 18))

    for n, pair in enumerate(pairs):
        landed(back_mid.at[pair], 11 + n)
        (to_zc if n else to_y)(back_mid.at[pair], back_got.at[pair], 19 + n)

    landed(wa_got, 17)
    sums = added(wa_got, nz)
    for k in range(ny):
        fill(wa2.at[k], sums[k * ra : (k + 1) * ra, :])
    along_y(lambda k: wa2.at[k], lambda k: wa2_got.at[k], 24)
    keep(wa2.at[y], wa2_got.at[y], 24)
    landed(wb_got, 18)
    sums = added(wb_got, ny)
    for k in range(nz):
        fill(wb2.at[k, 0:rb], sums[k * rb : (k + 1) * rb, :])
        fill(wb2.at[k, rb : rb + 1], sums[pb : pb + 1, :])
    along_z(lambda k: wb2.at[k], lambda k: wb2_got.at[k], 25)
    keep(wb2.at[z], wb2_got.at[z], 25)
    if ny > 1:
        pending.append((wa2.at[0 : ny - 1], 24))
    if nz > 1:
        pending.append((wb2.at[0 : nz - 1], 25))

    def to_x(src, dst, n):
        for j in far_first(nx):
            push(src, dst, n, at_x((v + j) % nx))

        keep(src, dst, n)
        for _ in range(nx - 1):
            pending.append((src, n))

    def plane(r):
        return all_f.at[v, r]

    landed(bgeo_mid, 16)
    to_y(bgeo_mid, bgeo_got, 23)
    older = len(pending)
    landed(back_got.at[0:half], 19)
    to_x(back_got.at[0], plane(0), 26)

    landed(wa2_got, 24)
    landed(wb2_got, 25)
    wq[0:ra] = added(wa2_got, ny)
    wq[ra:] = added(wb2_got, nz)
    to_x(wq, wq_got.at[v], 31)
    for r in range(1, RANKS):
        if r == half:
            landed(back_got.at[half:RANKS], 20)
        to_x(back_got.at[r], plane(r), 26 + r)
        if r == 1:
            landed(bgeo_got, 23)
            own_g[...] = turned(rows_of(bgeo_got, strips))
            to_x(own_g, all_g.at[v], 30)

    if nx > 1:
        landed(asked_all.at[0 : nx - 1], 3)
    slot_at = iota((block, 1), 0).astype(F32).astype(BF16)

    def geometry_of(r):
        return three(jnp.concatenate([shared_g[k][8 * r : 8 * r + 8, :] for k in range(nx)], axis=1))

    def scatter(r):
        asks = jnp.concatenate([asked_all[k][r : r + 1, :] for k in range(nx)], axis=1)
        came_g = geometry_of(r)
        high, low = split(jnp.concatenate([rows_of(all_f.at[k, r], strips) for k in range(nx)], axis=0))
        came = jnp.concatenate([high, low], axis=1)

        @pl.loop(0, prims // rows)
        def _(i):
            here = pl.ds(pl.multiple_of(i * rows, rows), rows)
            base = (i * rows).astype(F32)
            hits = jnp.concatenate(
                [
                    jnp.where(
                        slot_at == (asks - (base + float(k * block))).astype(BF16),
                        jnp.ones((), BF16),
                        jnp.zeros((), BF16),
                    )
                    for k in range(rows // block)
                ],
                axis=0,
            )
            both = mm(hits, came)
            both = both[:, 0:width] + both[:, width:]
            found = mm(came_g, hits, 1, 1)
            found = found[0:8] + found[8:16] + found[16:24]
            if r:
                total[here, :] += both
                total_g[i] += found
            else:
                total[here, :] = both
                total_g[i] = found

    drain(older)
    landed(wq_got, 31)
    sums = added(wq_got, nx)
    b_total[...] = sums[ra + rb]
    save_b = pltpu.make_async_copy(b_total, bias_out, local.at[4])
    save_b.start()
    wa3[y] = sums[0:ra]
    wb3[z] = sums[ra : ra + rb]
    along_y(lambda k: wa3.at[y], lambda k: wa3.at[k], 32)
    along_z(lambda k: wb3.at[z], lambda k: wb3.at[k], 33)
    if ny > 1:
        pending.append((wa3.at[0 : ny - 1], 32))
    if nz > 1:
        pending.append((wb3.at[0 : nz - 1], 33))

    landed(all_g, 30)
    shared_g = [all_g[k] for k in range(nx)]
    landed(all_f.at[:, 0], 26)
    scatter(0)

    if ny > 1:
        landed(wa3.at[0 : ny - 1], 32)
    if nz > 1:
        landed(wb3.at[0 : nz - 1], 33)

    def part_a(k):
        return weight_out.at[c, pl.ds(pl.multiple_of(k * pa, 8), pa)]

    def part_b(k):
        return weight_out.at[c, pl.ds(pl.multiple_of(rows_a + k * pb, 8), pb)]

    mine_a[...] = rows_of(wa3, pa)
    mine_b[...] = rows_of(wb3, pb)
    along_z(lambda k: mine_a, part_a, 34)
    along_y(lambda k: mine_b, part_b, 35)
    keep(mine_a, part_a(z), 34)
    keep(mine_b, part_b(y), 35)
    for _ in range(nz - 1):
        pending.append((mine_a, 34))
    for _ in range(ny - 1):
        pending.append((mine_b, 35))

    landed(all_f.at[:, 1], 27)
    scatter(1)
    landed(all_f.at[:, 2], 28)
    scatter(2)
    landed(all_f.at[:, 3], 29)
    scatter(3)
    save_f = pltpu.make_async_copy(total, feature_out, local.at[3])
    save_f.start()
    for i in range(prims // rows):
        g_total[:, i * rows : (i + 1) * rows] = total_g[i][0:7]
    save_g = pltpu.make_async_copy(g_total, geometry_out, local.at[2])
    save_g.start()

    drain()
    landed(weight_out.at[c, 0:rows_a], 34)
    landed(weight_out.at[c, rows_a:], 35)
    push(weight_out.at[c], weight_out.at[c], 36, other)
    pending.append((weight_out.at[0], 36))
    landed(weight_out.at[0], 36)
    drain()
    save_f.wait()
    save_g.wait()
    save_b.wait()


def decoder_rows(sizes):
    nx, ny, nz, nc, entries, prims, height = sizes
    rows = 9 * 128 // nc
    rows_a = rows * 5 // 9
    rows_b = rows - rows_a
    return rows_a, rows_b, rows_a // nz, rows_b // ny, rows_a // nz // ny, rows_b // nz // ny


def passing(count, *refs):
    moves = [pltpu.make_async_copy(refs[i], refs[count + i], refs[-1].at[i]) for i in range(count)]
    for move in moves:
        move.start()
    for move in moves:
        move.wait()


def hand_over(*arrays):
    any_ = pl.BlockSpec(memory_space=pl.ANY)
    return pl.pallas_call(
        functools.partial(passing, len(arrays)),
        name="hand_over",
        out_shape=tuple(jax.ShapeDtypeStruct(a.shape, a.dtype) for a in arrays),
        in_specs=[any_] * len(arrays),
        out_specs=(any_,) * len(arrays),
        scratch_shapes=[pltpu.SemaphoreType.DMA((len(arrays),))],
        compiler_params=pltpu.CompilerParams(vmem_limit_bytes=1024 * 1024),
    )(*arrays)


def per_device(sizes, *arrays):
    means, inv_scales, correlation, opacity, features, cameras, owners, slots, lengths, target, weights, bias = arrays
    nx, ny, nz, nc, entries, prims, height = sizes
    zc = nz * nc
    strips = ny * zc
    width = 128
    pixels = height * 16
    rows = min(prims, 512)
    rows_a, rows_b, pa, pb, ra, rb = decoder_rows(sizes)
    any_ = pl.BlockSpec(memory_space=pl.ANY)
    hbm = pl.BlockSpec(memory_space=pltpu.HBM)

    def f32(*shape):
        return pltpu.VMEM(shape, F32)

    def planes(n):
        return f32(n, zc, ny, 1, width)

    geometry, feature, weight, b_grad = pl.pallas_call(
        functools.partial(kernel, sizes),
        name="splat_step",
        out_shape=(
            jax.ShapeDtypeStruct((7, prims), F32),
            jax.ShapeDtypeStruct((prims, width), F32),
            jax.ShapeDtypeStruct((nc, rows_a + rows_b, width), F32),
            jax.ShapeDtypeStruct((1, width), F32),
        ),
        in_specs=[hbm] * 7 + [pl.BlockSpec(memory_space=pltpu.SMEM)] + [hbm] * 4,
        out_specs=(any_,) * 4,
        scratch_shapes=[
            pltpu.VMEM((1, entries), jnp.int32), pltpu.VMEM((1, entries), jnp.int32), f32(1, width),
            f32(1, 2, 4),
            f32(prims, width), f32(pixels, width), f32(9 * width, width), f32(7, prims),
            pltpu.VMEM((width, prims), BF16), pltpu.VMEM((prims, 2 * width), BF16),
            pltpu.VMEM((9 * width, 2 * width), BF16), pltpu.VMEM((3, 2, width, 3 * width), BF16),
            pltpu.VMEM((RANKS * strips, prims), BF16), f32(2, 16, width),
            planes(1), planes(1), planes(1), f32(nx, 8, strips),
            planes(1), planes(1), planes(1), planes(RANKS), planes(RANKS), planes(RANKS),
            f32(pixels + 64, width), planes(RANKS), planes(RANKS), planes(RANKS), planes(1), planes(1), planes(1),
            f32(nx, RANKS, zc, ny, 1, width), f32(nx, 8 * RANKS, strips), f32(8 * RANKS, strips),
            f32(prims, width), f32(prims // rows, 8, rows), f32(9 * width, width),
            f32(nc, rows_a + rows_b + 8 * ny, width), f32(rows_a + rows_b + 8 * ny, width),
            f32(nz, pa, width), f32(nz, pa, width), f32(ny, pb + 8, width), f32(ny, pb + 8, width),
            f32(ny, ra, 1, width), f32(ny, ra, 1, width), f32(nz, rb + 1, 1, width), f32(nz, rb + 1, 1, width),
            f32(ra + rb + 1, 1, width), f32(nx, ra + rb + 1, 1, width),
            f32(ny, ra, 1, width), f32(nz, rb, 1, width), f32(pa, width), f32(pb, width), f32(7, prims), f32(1, width),
            pltpu.SemaphoreType.DMA((46,)), pltpu.SemaphoreType.DMA((46,)), pltpu.SemaphoreType.DMA((13,)),
        ],
        compiler_params=pltpu.CompilerParams(
            collective_id=0, has_side_effects=True, vmem_limit_bytes=VMEM_LIMIT
        ),
    )(
        *[a if n == 7 else pltpu.with_memory_space_constraint(a, pltpu.HBM) for n, a in enumerate((
        means, inv_scales, correlation.reshape(1, prims), opacity.reshape(1, prims), cameras,
        owners.reshape(1, entries), slots.reshape(1, entries), lengths.reshape(1, 1), bias.reshape(1, width),
        features, target.reshape(pixels, width), weights.reshape(9 * width, width),
        ))],
    )
    geometry, feature, weight, b_grad = hand_over(geometry, feature, weight.reshape(9 * width, width), b_grad)
    return geometry, feature, weight.reshape(3, 3, width, width), b_grad.reshape(width)


def built(mesh, ny, nz, nc, entries, prims, height):
    nx = mesh.shape["view"]
    finer = Mesh(mesh.devices.reshape(nx, ny, nz, nc), ("view",) + STRIP)
    return jax.shard_map(
        functools.partial(per_device, (nx, ny, nz, nc, entries, prims, height)),
        mesh=finer,
        in_specs=(
            P(None, STRIP),
            P(None, STRIP),
            P(STRIP),
            P(STRIP),
            P(STRIP, None),
            P("view", None, None),
            P("view", STRIP, None, None),
            P("view", STRIP, None),
            P("view", STRIP),
            P("view", STRIP, None, None),
            P(),
            P(),
        ),
        out_specs=(P(None, STRIP), P(STRIP, None), P(), P()),
        check_vma=False,
    )


def solution(mesh):
    return built(mesh, 8, 8, 2, 256, 2048, 16)
```

```python
import functools

import jax
import jax.numpy as jnp
from jax import lax
from jax.experimental import pallas as pl
from jax.experimental.pallas import tpu as pltpu
from jax.sharding import Mesh
from jax.sharding import PartitionSpec as P

STRIP = ("strip_0", "strip_1", "strip_2")
MESH = pl.DeviceIdType.MESH
F32 = jnp.float32
BF16 = jnp.bfloat16
VMEM_LIMIT = 24 * 1024 * 1024
RANKS = 4


def iota(shape, dim):
    return lax.broadcasted_iota(jnp.int32, shape, dim)


def mm(a, b, ca=1, cb=0):
    return lax.dot_general(a, b, (((ca,), (cb,)), ((), ())), preferred_element_type=F32)


def split(x):
    high = x.astype(BF16)
    return high, (x - high.astype(F32)).astype(BF16)


def split3(x):
    high = x.astype(BF16)
    rest = x - high.astype(F32)
    mid = rest.astype(BF16)
    return high, mid, (rest - mid.astype(F32)).astype(BF16)


def far_first(n):
    return sorted(range(1, n), key=lambda j: -min(j, n - j))


def rows_of(ref, n):
    return ref.reshape(n, ref.shape[-1])[...]


def fill(ref, value):
    ref.reshape(*value.shape)[...] = value


def kernel(
    sizes,
    means, inv_scales, correlation, opacity, cameras_hbm, owners_hbm, slots_hbm, lengths, bias_hbm,
    features_hbm, target_hbm, weights_hbm,
    geometry_out, feature_out, weight_out, bias_out,
    owners, slots, bias, cameras, feat, targ, wts, table, g_parts, f_parts, w_parts, w_turned, onehot, halo_t,
    req, req_mid, req_got, asked_all,
    geo, geo_mid, geo_got, fea, fea_mid, fea_got,
    image, back, back_mid, back_got, bgeo, bgeo_mid, bgeo_got, all_f, all_g, own_g,
    total, total_g, wl, wx, wc, wa, wa_got, wb, wb_got, wa2, wa2_got, wb2, wb2_got, wq, wq_got, wa3, wb3, mine_a, mine_b, g_total, b_total,
    send, recv, local,
):
    nx, ny, nz, nc, entries, prims, height = sizes
    zc_count = nz * nc
    strips = ny * zc_count
    places = RANKS * strips
    width = 128
    pixels = height * 16
    extended = pixels + 32
    v = lax.axis_index("view")
    y = lax.axis_index("strip_0")
    z = lax.axis_index("strip_1")
    c = lax.axis_index("strip_2")
    zc = z * nc + c
    strip = y * zc_count + zc

    def at_zc(k):
        return (v, y, k // nc, k % nc)

    def at_y(k):
        return (v, k, z, c)

    def at_x(k):
        return (k, y, z, c)

    def at_strip(k):
        return (v, k // zc_count, (k % zc_count) // nc, k % nc)

    up = at_strip((strip + strips - 1) % strips)
    down = at_strip((strip + 1) % strips)

    def push(src, dst, n, device):
        pltpu.make_async_remote_copy(
            src_ref=src, dst_ref=dst, send_sem=send.at[n], recv_sem=recv.at[n],
            device_id=device, device_id_type=MESH,
        ).start()

    def keep(src, dst, n):
        pltpu.make_async_copy(src, dst, recv.at[n]).start()

    def landed(ref, n):
        pltpu.make_async_copy(ref, ref, recv.at[n]).wait()

    def sent(ref, n):
        pltpu.make_async_copy(ref, ref, send.at[n]).wait()

    pending = []

    def drain(count=None):
        for ref, n in pending[:count]:
            sent(ref, n)
        del pending[:count]

    def to_zc(src, dst, n):
        for j in far_first(zc_count):
            k = (zc + j) % zc_count
            push(src.at[:, k], dst.at[:, zc], n, at_zc(k))

        keep(src.at[:, zc], dst.at[:, zc], n)
        if zc_count > 1:
            pending.append((src.at[:, 0 : zc_count - 1], n))

    def to_y(src, dst, n):
        for j in far_first(ny):
            k = (y + j) % ny
            push(src.at[:, :, k], dst.at[:, :, y], n, at_y(k))

        keep(src.at[:, :, y], dst.at[:, :, y], n)
        if ny > 1:
            pending.append((src.at[:, :, 0 : ny - 1], n))

    load_o = pltpu.make_async_copy(owners_hbm, owners, local.at[5])
    load_s = pltpu.make_async_copy(slots_hbm, slots, local.at[6])
    load_b = pltpu.make_async_copy(bias_hbm, bias, local.at[7])
    load_c = pltpu.make_async_copy(cameras_hbm, cameras, local.at[12])
    load_g = [
        pltpu.make_async_copy(ref, table.at[a:b], local.at[8 + i])
        for i, (ref, a, b) in enumerate(
            ((means, 0, 3), (inv_scales, 3, 5), (correlation, 5, 6), (opacity, 6, 7))
        )
    ]
    load_o.start()
    load_s.start()
    load_f = pltpu.make_async_copy(features_hbm, feat, local.at[0])
    load_t = pltpu.make_async_copy(target_hbm, targ, local.at[1])
    load_w = pltpu.make_async_copy(weights_hbm, wts, local.at[2])

    barrier = pltpu.get_barrier_semaphore()

    for j in far_first(zc_count):
        pl.semaphore_signal(barrier, inc=1, device_id=at_zc((zc + j) % zc_count), device_id_type=MESH)

    for j in far_first(ny):
        pl.semaphore_signal(barrier, inc=1, device_id=at_y((y + j) % ny), device_id_type=MESH)

    for j in far_first(nx):
        pl.semaphore_signal(barrier, inc=1, device_id=at_x((v + j) % nx), device_id_type=MESH)

    pl.semaphore_signal(barrier, inc=1, device_id=up, device_id_type=MESH)
    pl.semaphore_signal(barrier, inc=1, device_id=down, device_id_type=MESH)

    def column(row):
        n = row.shape[1]
        same = iota((n, n), 0) == iota((n, n), 1)
        return jnp.sum(jnp.where(same, jnp.broadcast_to(row, (n, n)), 0.0), axis=1, keepdims=True)

    first = iota((entries, entries), 0)
    second = iota((entries, entries), 1)
    load_o.wait()
    owner = owners[...]
    home = ((owner % zc_count) * ny + owner // zc_count).astype(F32)
    home_col = column(home)
    alike = home_col == home
    rank_row = jnp.sum(jnp.where(alike & (first < second), 1.0, 0.0), axis=0, keepdims=True)
    at_home = jnp.where(iota((strips, entries), 0).astype(F32) == home, 1.0, 0.0).astype(BF16)
    load_s.wait()
    slot = slots[...].astype(F32)
    slot_high = jnp.floor(slot * (1.0 / 64.0))
    slot_low = slot - 64.0 * slot_high
    row_at = iota((width, entries), 0).astype(F32)
    sought = jnp.where(row_at == rank_row, slot_high, 0.0) + jnp.where(row_at - 8.0 == rank_row, slot_low, 0.0)
    sought = mm(at_home, sought.astype(BF16), 1, 1)
    fill(req, sought * 64.0 + pltpu.roll(sought, width - 8, 1))

    pl.semaphore_wait(barrier, zc_count + ny + nx - 3 + 2)

    to_zc(req, req_mid, 0)
    for load in load_g + [load_f, load_w, load_t, load_b, load_c]:
        load.start()
    push(target_hbm.at[0:16], halo_t.at[1], 1, up)
    push(target_hbm.at[pixels - 16 : pixels], halo_t.at[0], 1, down)
    pending.append((halo_t, 1))

    for load in load_g:
        load.wait()
    whole = jnp.concatenate([table[...], jnp.zeros((1, prims), F32)], axis=0)
    g_high, g_mid, g_low = (part.astype(F32) for part in split3(whole))
    g_parts[...] = jnp.concatenate(
        [g_high] * RANKS + [g_mid] * RANKS + [g_low] * RANKS + [jnp.zeros((32, prims), F32)], axis=0
    ).astype(BF16)
    load_f.wait()
    rows = min(prims, 512)

    @pl.loop(0, prims // rows)
    def _(i):
        here = pl.ds(pl.multiple_of(i * rows, rows), rows)
        high, low = split(feat[here, :])
        f_parts[here, 0:width] = high
        f_parts[here, width : 2 * width] = low

    landed(req_mid, 0)
    to_y(req_mid, req_got, 2)

    load_w.wait()
    for tap in range(9):
        high, low = split(wts[tap * width : (tap + 1) * width, :])
        w_parts[tap * width : (tap + 1) * width, 0:width] = high
        w_parts[tap * width : (tap + 1) * width, width : 2 * width] = low
        a, b = 2 - tap // 3, 2 - tap % 3
        w_turned[a, 0, :, b * width : (b + 1) * width] = high
        w_turned[a, 1, :, b * width : (b + 1) * width] = low
    load_t.wait()
    load_b.wait()
    load_c.wait()
    rank_col = jnp.sum(jnp.where(alike & (second < first), 1.0, 0.0), axis=1, keepdims=True)
    place_row = rank_row * float(strips) + home
    place_col = rank_col * float(strips) + home_col
    to_place = jnp.where(iota((places, entries), 0).astype(F32) == place_row, 1.0, 0.0).astype(BF16)
    from_place = jnp.where(iota((entries, places), 1).astype(F32) == place_col, 1.0, 0.0).astype(BF16)
    before = jnp.where(first < second, 1.0, 0.0).astype(BF16)
    behind = jnp.where(first > second, 1.0, 0.0).astype(BF16)

    landed(req_got, 2)
    asked = rows_of(req_got, strips)
    block = min(prims, 256)
    ident = iota((1, block), 1).astype(F32).astype(BF16)
    packed = jnp.zeros((strips, width), F32)
    lanes = iota((strips, width), 1)
    for r in range(RANKS):
        for k in range(prims // block):
            near = (asked[:, r : r + 1] - float(k * block)).astype(BF16)
            onehot[r * strips : (r + 1) * strips, k * block : (k + 1) * block] = jnp.where(
                ident == near, jnp.ones((), BF16), jnp.zeros((), BF16)
            )
    for r in range(RANKS):
        found = mm(onehot[r * strips : (r + 1) * strips, :], g_parts[...], 1, 1)
        packed = packed + jnp.where((lanes % 32) // 8 == r, found, 0.0)

    def folded(x):
        x = x + pltpu.roll(x, width - 32, 1) + pltpu.roll(x, width - 64, 1)
        return jnp.where(lanes < 32, x, 0.0)

    fill(geo, folded(packed))
    to_zc(geo, geo_mid, 4)

    half = RANKS // 2
    pairs = (slice(0, half), slice(half, RANKS))
    for n, pair in enumerate(pairs):
        for r in range(pair.start, pair.stop):
            found = mm(onehot[r * strips : (r + 1) * strips, :], f_parts[...])
            fill(fea.at[r], found[:, 0:width] + found[:, width : 2 * width])
        (to_y if n else to_zc)(fea.at[pair], fea_mid.at[pair], 37 + n)
    square = jnp.concatenate([asked, jnp.zeros((width - strips, width), F32)], axis=0) if strips < width else asked
    asked_rows = jnp.transpose(square)[0:8, 0:strips]
    asked_all[v] = asked_rows

    for j in far_first(nx):
        push(asked_all.at[v], asked_all.at[v], 3, at_x((v + j) % nx))

    if nx > 1:
        pending.append((asked_all.at[0 : nx - 1], 3))

    landed(geo_mid, 4)
    to_y(geo_mid, geo_got, 7)
    for n, pair in enumerate(pairs):
        landed(fea_mid.at[pair], 37 + n)
        (to_zc if n else to_y)(fea_mid.at[pair], fea_got.at[pair], 41 + n)

    landed(geo_got, 7)

    def turned(x):
        x = jnp.concatenate([x, jnp.zeros((width - strips, width), F32)], axis=0) if strips < width else x
        return jnp.transpose(x)[0 : 8 * RANKS, 0:strips]

    def three(x):
        return jnp.concatenate([part.astype(F32) for part in split3(x)], axis=0).astype(BF16)

    spread = mm(three(turned(rows_of(geo_got, strips))), at_home)
    n8 = 8 * RANKS
    spread = spread[0:n8] + spread[n8 : 2 * n8] + spread[2 * n8 : 3 * n8]
    g = jnp.zeros((8, entries), F32)
    for r in range(RANKS):
        g = g + jnp.where(rank_row == float(r), spread[8 * r : 8 * r + 8, :], 0.0)

    def cam(axis, k):
        return cameras[0, axis : axis + 1, k : k + 1]

    def center(axis):
        return 8.0 + 4.0 * (
            cam(axis, 0) * g[0:1] + cam(axis, 1) * g[1:2] + cam(axis, 2) * g[2:3] + cam(axis, 3)
        )

    pixel = iota((pixels, 1), 0)
    across = (pixel % 16).astype(F32) + 0.5
    downward = (pixel // 16).astype(F32) + 0.5
    du = across - center(0)
    dv = downward - center(1)
    a = g[3:4] * du
    b = g[4:5] * dv
    skew = g[5:6]
    grown = jnp.exp(-0.5 * (a * a + 2.0 * skew * a * b + b * b))
    solid = 1.0 / (1.0 + jnp.exp(-g[6:7]))
    raw = solid * grown
    alive = jnp.where(iota((1, entries), 1) < lengths[0, 0], 1.0, 0.0)
    cover = jnp.minimum(raw, 0.99) * alive
    fades = jnp.log(1.0 - cover)
    f_high, f_mid, f_low = split3(fades)
    through = jnp.exp(mm(f_high, before) + mm(f_mid, before) + mm(f_low, before))
    weight = cover * through
    weight_high, weight_low = split(weight)

    weight_t_high = jnp.transpose(weight_high.astype(F32)).astype(BF16)
    weight_t_low = jnp.transpose(weight_low.astype(F32)).astype(BF16)
    for n, pair in enumerate(pairs):
        landed(fea_got.at[pair], 41 + n)
    high, low = split(rows_of(fea_got, places))
    listed = mm(from_place, jnp.concatenate([high, low], axis=1)).astype(BF16)
    both = mm(weight_high, listed)
    tile = both[:, 0:width] + both[:, width:] + mm(weight_low, listed[:, 0:width])
    image[32 : 32 + pixels, :] = tile

    push(image.at[32:64], image.at[32 + pixels : 64 + pixels], 10, up)
    push(image.at[pixels : 32 + pixels], image.at[0:32], 10, down)
    pending.append((image.at[0:64], 10))

    def sideways(x):
        n = x.shape[0]
        col = iota((n, 1), 0) % 16
        left = jnp.where(col == 0, 0.0, pltpu.roll(x, 1, 0))
        right = jnp.where(col == 15, 0.0, pltpu.roll(x, n - 1, 0))
        return split(jnp.concatenate([left, x, right], axis=1))

    def taps(i):
        return w_parts[i * 3 * width : (i + 1) * 3 * width, :]

    def product(high, low, part):
        both = mm(high, part)
        return both[:, 0:width] + (both[:, width:] + mm(low, part[:, 0:width]))

    edge = jnp.zeros((32, width), F32)
    pic_high, pic_low = sideways(jnp.concatenate([edge, tile, edge], axis=0))
    decoded = jnp.zeros((extended, width), F32)
    for i in range(3):
        here = slice(i * 16, i * 16 + extended)
        decoded = decoded + product(pic_high[here, :], pic_low[here, :], taps(i))
    decoded = decoded + bias[...]
    pic_t_high = jnp.transpose(pic_high.astype(F32)).astype(BF16)
    pic_t_low = jnp.transpose(pic_low.astype(F32)).astype(BF16)
    drain()
    landed(halo_t, 1)
    aim = jnp.concatenate([halo_t[0], targ[...], halo_t[1]], axis=0)
    decoded = decoded - aim

    landed(image.at[0:64], 10)
    has_up = strip > 0
    has_down = strip < strips - 1
    beyond = jnp.concatenate([image[0:32, :], image[32 + pixels :, :]], axis=0)
    known = jnp.where(iota((64, 1), 0) < 32, has_up.astype(F32), has_down.astype(F32)) > 0.5
    out_high, out_low = sideways(jnp.where(known, beyond, 0.0))
    top = product(out_high[0:32, :], out_low[0:32, :], taps(0))
    mid = product(out_high[16:48, :], out_low[16:48, :], taps(1))
    low = product(out_high[32:64, :], out_low[32:64, :], taps(2))
    decoded = jnp.concatenate(
        [
            decoded[0:16] + (top[0:16] + mid[0:16]),
            decoded[16:32] + top[16:32],
            decoded[32 : extended - 32],
            decoded[extended - 32 : extended - 16] + low[0:16],
            decoded[extended - 16 :] + (low[16:32] + mid[16:32]),
        ],
        axis=0,
    )
    rows_at = iota((extended, 1), 0)
    inside = ((rows_at >= 16) | has_up) & ((rows_at < 16 + pixels) | has_down)
    residual = jnp.where(inside, decoded, 0.0)
    res_high, res_low = sideways(residual)
    own = residual[16 : 16 + pixels, :]
    shifted = []
    for i in range(3):
        shifted.append(
            jnp.concatenate(
                [jnp.zeros(((i + 1) * 16, width), F32), own, jnp.zeros((64 - (i + 1) * 16, width), F32)], axis=0
            )
        )
    own_high, own_low = split(jnp.concatenate(shifted, axis=1))
    w_grad = mm(pic_t_high, own_high) + (mm(pic_t_high, own_low) + mm(pic_t_low, own_high))
    next_high = jnp.concatenate([own_high[16:32], own_high[pixels + 32 : pixels + 48]], axis=0)
    next_low = jnp.concatenate([own_low[16:32], own_low[pixels + 32 : pixels + 48]], axis=0)
    near_high, near_low = out_high[16:48], out_low[16:48]
    w_grad = w_grad + (mm(near_high, next_high, 0, 0) + (mm(near_high, next_low, 0, 0) + mm(near_low, next_high, 0, 0)))
    for i in range(3):
        wl[i * 3 * width : (i + 1) * 3 * width, :] = w_grad[:, i * width : (i + 1) * width]
    b_grad = jnp.broadcast_to(jnp.sum(own, axis=0, keepdims=True), (8, width))
    rows_a, rows_b, pa, pb, ra, rb = decoder_rows(sizes)
    core_rows = rows_a + rows_b
    for k in range(nc):
        base = k * core_rows
        wx[k, 0:rows_a, :] = wl[base : base + rows_a, :]
        for i in range(ny):
            at = rows_a + i * (pb + 8)
            wx[k, at : at + pb, :] = wl[base + rows_a + i * pb : base + rows_a + (i + 1) * pb, :]
            wx[k, at + pb : at + pb + 8, :] = b_grad
    other = (v, y, z, 1 - c)
    push(wx.at[1 - c, 0:rows_a], wc.at[0:rows_a], 15, other)
    push(wx.at[1 - c, rows_a:], wc.at[rows_a:], 45, other)
    pending.append((wc.at[0:rows_a], 15))
    pending.append((wc.at[rows_a:], 45))

    grad = jnp.zeros((pixels, width), F32)
    for i in range(3):
        here = slice(i * 16, i * 16 + pixels)
        grad = grad + (
            mm(res_high[here, :], w_turned[i, 0], 1, 1)
            + (mm(res_high[here, :], w_turned[i, 1], 1, 1) + mm(res_low[here, :], w_turned[i, 0], 1, 1))
        )
    grad_high, grad_low = split(grad)

    both = mm(weight_t_high, jnp.concatenate([grad_high, grad_low], axis=1))
    f_grad = both[:, 0:width] + (both[:, width:] + mm(weight_t_low, grad_high))
    high, low = split(f_grad)
    f_grad = jnp.concatenate([high, low], axis=1)
    for r in range(RANKS):
        both = mm(to_place[r * strips : (r + 1) * strips, :], f_grad)
        fill(back.at[r], both[:, 0:width] + both[:, width:])
    for n, pair in enumerate(pairs):
        (to_y if n else to_zc)(back.at[pair], back_mid.at[pair], 11 + n)


    def along_z(src, dst, n):
        for j in far_first(nz):
            k = (z + j) % nz
            push(src(k), dst(z), n, (v, y, k, c))

    def along_y(src, dst, n):
        for j in far_first(ny):
            k = (y + j) % ny
            push(src(k), dst(y), n, at_y(k))

    def added(ref, n):
        sums = ref[0]
        for k in range(1, n):
            sums = sums + ref[k]
        return sums

    landed(wc.at[0:rows_a], 15)
    wa[...] = (wx[c, 0:rows_a, :] + wc[0:rows_a, :]).reshape(nz, pa, width)
    along_z(lambda k: wa.at[k], lambda k: wa_got.at[k], 17)
    keep(wa.at[z], wa_got.at[z], 17)

    d_weight = mm(jnp.concatenate([grad_high, grad_high], axis=1), listed, 1, 1) + mm(
        grad_low, listed[:, 0:width], 1, 1
    )
    f_high, f_mid, f_low = split3(d_weight * weight)
    later = mm(f_high, behind) + mm(f_mid, behind) + mm(f_low, behind)
    d_cover = d_weight * through - later / (1.0 - cover)
    d_raw = jnp.where(raw < 0.99, d_cover, 0.0) * alive
    d_grown = d_raw * raw
    u = (a + skew * b) * d_grown
    w = (b + skew * a) * d_grown

    def summed(x):
        return jnp.sum(x, axis=0, keepdims=True)

    d_col = 4.0 * g[3:4] * summed(u)
    d_row = 4.0 * g[4:5] * summed(w)
    parts = [cam(0, k) * d_col + cam(1, k) * d_row for k in range(3)]
    parts += [-summed(u * du), -summed(w * dv), -summed(d_grown * a * b), summed(d_grown) * (1.0 - solid)]
    parts.append(jnp.zeros((1, entries), F32))
    g_grad = jnp.concatenate(parts, axis=0)
    by_rank = jnp.concatenate([jnp.where(rank_row == float(r), g_grad, 0.0) for r in range(RANKS)], axis=0)
    by_rank = jnp.concatenate([part.astype(F32) for part in split3(by_rank)] + [jnp.zeros((32, entries), F32)], axis=0)
    fill(bgeo, folded(mm(at_home, by_rank.astype(BF16), 1, 1)))
    landed(wc.at[rows_a:], 45)
    wb[...] = (wx[c, rows_a:, :] + wc[rows_a:, :]).reshape(ny, pb + 8, width)
    along_y(lambda k: wb.at[k], lambda k: wb_got.at[k], 18)
    keep(wb.at[y], wb_got.at[y], 18)
    to_zc(bgeo, bgeo_mid, 16)
    if nz > 1:
        pending.append((wa.at[0 : nz - 1], 17))
    if ny > 1:
        pending.append((wb.at[0 : ny - 1], 18))

    for n, pair in enumerate(pairs):
        landed(back_mid.at[pair], 11 + n)
        (to_zc if n else to_y)(back_mid.at[pair], back_got.at[pair], 19 + n)

    landed(wa_got, 17)
    sums = added(wa_got, nz)
    for k in range(ny):
        fill(wa2.at[k], sums[k * ra : (k + 1) * ra, :])
    along_y(lambda k: wa2.at[k], lambda k: wa2_got.at[k], 24)
    keep(wa2.at[y], wa2_got.at[y], 24)
    landed(wb_got, 18)
    sums = added(wb_got, ny)
    for k in range(nz):
        fill(wb2.at[k, 0:rb], sums[k * rb : (k + 1) * rb, :])
        fill(wb2.at[k, rb : rb + 1], sums[pb : pb + 1, :])
    along_z(lambda k: wb2.at[k], lambda k: wb2_got.at[k], 25)
    keep(wb2.at[z], wb2_got.at[z], 25)
    if ny > 1:
        pending.append((wa2.at[0 : ny - 1], 24))
    if nz > 1:
        pending.append((wb2.at[0 : nz - 1], 25))

    def to_x(src, dst, n):
        for j in far_first(nx):
            push(src, dst, n, at_x((v + j) % nx))

        keep(src, dst, n)
        for _ in range(nx - 1):
            pending.append((src, n))

    def plane(r):
        return all_f.at[v, r]

    landed(bgeo_mid, 16)
    to_y(bgeo_mid, bgeo_got, 23)
    older = len(pending)
    landed(back_got.at[0:half], 19)
    to_x(back_got.at[0], plane(0), 26)

    landed(wa2_got, 24)
    landed(wb2_got, 25)
    wq[0:ra] = added(wa2_got, ny)
    wq[ra:] = added(wb2_got, nz)
    to_x(wq, wq_got.at[v], 31)
    for r in range(1, RANKS):
        if r == half:
            landed(back_got.at[half:RANKS], 20)
        to_x(back_got.at[r], plane(r), 26 + r)
        if r == 1:
            landed(bgeo_got, 23)
            own_g[...] = turned(rows_of(bgeo_got, strips))
            to_x(own_g, all_g.at[v], 30)

    if nx > 1:
        landed(asked_all.at[0 : nx - 1], 3)
    slot_at = iota((block, 1), 0).astype(F32).astype(BF16)

    def geometry_of(r):
        return three(jnp.concatenate([shared_g[k][8 * r : 8 * r + 8, :] for k in range(nx)], axis=1))

    blocks = prims // rows

    def scatter(r, start=0, end=blocks):
        asks = jnp.concatenate([asked_all[k][r : r + 1, :] for k in range(nx)], axis=1)
        came_g = geometry_of(r)
        high, low = split(jnp.concatenate([rows_of(all_f.at[k, r], strips) for k in range(nx)], axis=0))
        came = jnp.concatenate([high, low], axis=1)

        @pl.loop(start, end)
        def _(i):
            here = pl.ds(pl.multiple_of(i * rows, rows), rows)
            base = (i * rows).astype(F32)
            hits = jnp.concatenate(
                [
                    jnp.where(
                        slot_at == (asks - (base + float(k * block))).astype(BF16),
                        jnp.ones((), BF16),
                        jnp.zeros((), BF16),
                    )
                    for k in range(rows // block)
                ],
                axis=0,
            )
            both = mm(hits, came)
            both = both[:, 0:width] + both[:, width:]
            found = mm(came_g, hits, 1, 1)
            found = found[0:8] + found[8:16] + found[16:24]
            if r:
                total[here, :] += both
                total_g[i] += found
            else:
                total[here, :] = both
                total_g[i] = found

    drain(older)
    landed(wq_got, 31)
    sums = added(wq_got, nx)
    b_total[...] = sums[ra + rb]
    save_b = pltpu.make_async_copy(b_total, bias_out, local.at[4])
    save_b.start()
    wa3[y] = sums[0:ra]
    wb3[z] = sums[ra : ra + rb]
    along_y(lambda k: wa3.at[y], lambda k: wa3.at[k], 32)
    along_z(lambda k: wb3.at[z], lambda k: wb3.at[k], 33)
    if ny > 1:
        pending.append((wa3.at[0 : ny - 1], 32))
    if nz > 1:
        pending.append((wb3.at[0 : nz - 1], 33))

    landed(all_g, 30)
    shared_g = [all_g[k] for k in range(nx)]
    landed(all_f.at[:, 0], 26)
    scatter(0)

    if ny > 1:
        landed(wa3.at[0 : ny - 1], 32)
    if nz > 1:
        landed(wb3.at[0 : nz - 1], 33)

    def part_a(k):
        return weight_out.at[c, pl.ds(pl.multiple_of(k * pa, 8), pa)]

    def part_b(k):
        return weight_out.at[c, pl.ds(pl.multiple_of(rows_a + k * pb, 8), pb)]

    mine_a[...] = rows_of(wa3, pa)
    mine_b[...] = rows_of(wb3, pb)
    along_z(lambda k: mine_a, part_a, 34)
    along_y(lambda k: mine_b, part_b, 35)
    keep(mine_a, part_a(z), 34)
    keep(mine_b, part_b(y), 35)
    for _ in range(nz - 1):
        pending.append((mine_a, 34))
    for _ in range(ny - 1):
        pending.append((mine_b, 35))

    landed(all_f.at[:, 1], 27)
    scatter(1)
    landed(all_f.at[:, 2], 28)
    scatter(2)
    landed(all_f.at[:, 3], 29)
    scatter(3, 0, blocks // 2)
    landed(weight_out.at[c, 0:rows_a], 34)
    landed(weight_out.at[c, rows_a:], 35)
    push(weight_out.at[c], weight_out.at[c], 36, other)
    pending.append((weight_out.at[0], 36))
    scatter(3, blocks // 2, blocks)
    save_f = pltpu.make_async_copy(total, feature_out, local.at[3])
    save_f.start()
    for i in range(prims // rows):
        g_total[:, i * rows : (i + 1) * rows] = total_g[i][0:7]
    save_g = pltpu.make_async_copy(g_total, geometry_out, local.at[2])
    save_g.start()

    drain()
    landed(weight_out.at[0], 36)
    drain()
    save_f.wait()
    save_g.wait()
    save_b.wait()


def decoder_rows(sizes):
    nx, ny, nz, nc, entries, prims, height = sizes
    rows = 9 * 128 // nc
    rows_a = rows * 5 // 9
    rows_b = rows - rows_a
    return rows_a, rows_b, rows_a // nz, rows_b // ny, rows_a // nz // ny, rows_b // nz // ny


def passing(count, *refs):
    moves = [pltpu.make_async_copy(refs[i], refs[count + i], refs[-1].at[i]) for i in range(count)]
    for move in moves:
        move.start()
    for move in moves:
        move.wait()


def hand_over(*arrays):
    any_ = pl.BlockSpec(memory_space=pl.ANY)
    return pl.pallas_call(
        functools.partial(passing, len(arrays)),
        name="hand_over",
        out_shape=tuple(jax.ShapeDtypeStruct(a.shape, a.dtype) for a in arrays),
        in_specs=[any_] * len(arrays),
        out_specs=(any_,) * len(arrays),
        scratch_shapes=[pltpu.SemaphoreType.DMA((len(arrays),))],
        compiler_params=pltpu.CompilerParams(vmem_limit_bytes=1024 * 1024),
    )(*arrays)


def per_device(sizes, *arrays):
    means, inv_scales, correlation, opacity, features, cameras, owners, slots, lengths, target, weights, bias = arrays
    nx, ny, nz, nc, entries, prims, height = sizes
    zc = nz * nc
    strips = ny * zc
    width = 128
    pixels = height * 16
    rows = min(prims, 512)
    rows_a, rows_b, pa, pb, ra, rb = decoder_rows(sizes)
    any_ = pl.BlockSpec(memory_space=pl.ANY)
    hbm = pl.BlockSpec(memory_space=pltpu.HBM)

    def f32(*shape):
        return pltpu.VMEM(shape, F32)

    def planes(n):
        return f32(n, zc, ny, 1, width)

    geometry, feature, weight, b_grad = pl.pallas_call(
        functools.partial(kernel, sizes),
        name="splat_step",
        out_shape=(
            jax.ShapeDtypeStruct((7, prims), F32),
            jax.ShapeDtypeStruct((prims, width), F32),
            jax.ShapeDtypeStruct((nc, rows_a + rows_b, width), F32),
            jax.ShapeDtypeStruct((1, width), F32),
        ),
        in_specs=[hbm] * 7 + [pl.BlockSpec(memory_space=pltpu.SMEM)] + [hbm] * 4,
        out_specs=(any_,) * 4,
        scratch_shapes=[
            pltpu.VMEM((1, entries), jnp.int32), pltpu.VMEM((1, entries), jnp.int32), f32(1, width),
            f32(1, 2, 4),
            f32(prims, width), f32(pixels, width), f32(9 * width, width), f32(7, prims),
            pltpu.VMEM((width, prims), BF16), pltpu.VMEM((prims, 2 * width), BF16),
            pltpu.VMEM((9 * width, 2 * width), BF16), pltpu.VMEM((3, 2, width, 3 * width), BF16),
            pltpu.VMEM((RANKS * strips, prims), BF16), f32(2, 16, width),
            planes(1), planes(1), planes(1), f32(nx, 8, strips),
            planes(1), planes(1), planes(1), planes(RANKS), planes(RANKS), planes(RANKS),
            f32(pixels + 64, width), planes(RANKS), planes(RANKS), planes(RANKS), planes(1), planes(1), planes(1),
            f32(nx, RANKS, zc, ny, 1, width), f32(nx, 8 * RANKS, strips), f32(8 * RANKS, strips),
            f32(prims, width), f32(prims // rows, 8, rows), f32(9 * width, width),
            f32(nc, rows_a + rows_b + 8 * ny, width), f32(rows_a + rows_b + 8 * ny, width),
            f32(nz, pa, width), f32(nz, pa, width), f32(ny, pb + 8, width), f32(ny, pb + 8, width),
            f32(ny, ra, 1, width), f32(ny, ra, 1, width), f32(nz, rb + 1, 1, width), f32(nz, rb + 1, 1, width),
            f32(ra + rb + 1, 1, width), f32(nx, ra + rb + 1, 1, width),
            f32(ny, ra, 1, width), f32(nz, rb, 1, width), f32(pa, width), f32(pb, width), f32(7, prims), f32(1, width),
            pltpu.SemaphoreType.DMA((46,)), pltpu.SemaphoreType.DMA((46,)), pltpu.SemaphoreType.DMA((13,)),
        ],
        compiler_params=pltpu.CompilerParams(
            collective_id=0, has_side_effects=True, vmem_limit_bytes=VMEM_LIMIT
        ),
    )(
        *[a if n == 7 else pltpu.with_memory_space_constraint(a, pltpu.HBM) for n, a in enumerate((
        means, inv_scales, correlation.reshape(1, prims), opacity.reshape(1, prims), cameras,
        owners.reshape(1, entries), slots.reshape(1, entries), lengths.reshape(1, 1), bias.reshape(1, width),
        features, target.reshape(pixels, width), weights.reshape(9 * width, width),
        ))],
    )
    geometry, feature, weight, b_grad = hand_over(geometry, feature, weight.reshape(9 * width, width), b_grad)
    return geometry, feature, weight.reshape(3, 3, width, width), b_grad.reshape(width)


def built(mesh, ny, nz, nc, entries, prims, height):
    nx = mesh.shape["view"]
    finer = Mesh(mesh.devices.reshape(nx, ny, nz, nc), ("view",) + STRIP)
    return jax.shard_map(
        functools.partial(per_device, (nx, ny, nz, nc, entries, prims, height)),
        mesh=finer,
        in_specs=(
            P(None, STRIP),
            P(None, STRIP),
            P(STRIP),
            P(STRIP),
            P(STRIP, None),
            P("view", None, None),
            P("view", STRIP, None, None),
            P("view", STRIP, None),
            P("view", STRIP),
            P("view", STRIP, None, None),
            P(),
            P(),
        ),
        out_specs=(P(None, STRIP), P(STRIP, None), P(), P()),
        check_vma=False,
    )


def solution(mesh):
    return built(mesh, 8, 8, 2, 256, 2048, 16)
```
